128 devices in a mesh: dp: 4 (over y), expert: 32 (over x, z, core).
Axes of the slice: x: 4, y: 4, z: 4, core: 2. Of those that a mesh axis runs over, the one named last changes fastest.
Arguments:
- tokens: bfloat16 [4, 2048, 2048], P(None, ('dp', 'expert')), may hold values from -6 to 6
- routes: int32 [4, 2048, 8], P(None, ('dp', 'expert')), may hold values from 0 to 31, as said below
- gates: float32 [4, 2048, 8], P(None, ('dp', 'expert')), may hold values from 0.05 to 1
- gate_up: bfloat16 [32, 2048, 1536], P('expert'), may hold values from -0.125 to 0.125
- down: bfloat16 [32, 2048, 768], P('expert'), may hold values from -0.21875 to 0.21875
- expert_load: int32 [8, 32], P('dp'), may hold values from 1 to 4095
- swap_pairs: int32 [16, 2], replicated, may hold values from 0 to 31, as said below
Outputs:
- mixed: float32 [4, 2048, 2048], P(None, ('dp', 'expert'))
- moved_gate_up: bfloat16 [32, 2048, 1536], P('expert')
- moved_down: bfloat16 [32, 2048, 768], P('expert')
- slot_share: float32 [32], P('expert')
The draws below stay inside these ranges and needn't reach their ends.
Inputs may be any that keep to these rules, and one draw needn't show every extreme that they name: `routes`: each row names 8 different experts. In every step the rows of one device name any expert at most 8 times, and in every step and every index of dp some expert is named exactly 8 times by the rows of every device. `swap_pairs`: the pairs name every slot exactly once.
All inputs are finite; a program needn't handle non-finite values.
Results may differ from the reference program's by a relative error of at most 0.0049.
Values may be sent and summed in bfloat16 or wider, within the bound.
A program may use at most 128 MiB of HBM per device.

```python
import math
import jax
import jax.numpy as jnp
from jax import lax

D = 2048
F = 768
TOP = 8
STEPS = 4
ROWS = 16
EXPERTS = 32
CAP = 8
TOKENS = 2048
DOMAINS = 8
PAIRS = 16


def label_table(label_key):
    return jax.random.permutation(label_key, EXPERTS)


def row_order(order_key):
    return jax.random.permutation(order_key, ROWS)


def draw_routes(key, part):
    cosets = EXPERTS // TOP
    blocks = STEPS * (TOKENS // ROWS)
    key_label, key_rows, key_coset, key_offset = jax.random.split(jax.random.fold_in(key, 11), 4)
    labels = jax.vmap(label_table)(jax.random.split(key_label, blocks // EXPERTS))
    labels = jnp.repeat(labels, EXPERTS, axis=0)
    orders = jax.vmap(row_order)(jax.random.split(key_rows, blocks))
    spare = jax.random.randint(key_coset, (blocks, ROWS), 1, max(cosets, 2))
    base_coset = jnp.where(jnp.arange(ROWS)[None, :] < CAP, 0, spare)
    coset = jnp.take_along_axis(base_coset, orders, axis=1)
    offsets = jax.random.randint(key_offset, (blocks, ROWS), 0, TOP)
    starting = coset + cosets * offsets
    position = (starting[:, :, None] + cosets * jnp.arange(TOP)[None, None, :]) % EXPERTS
    block_index = jnp.arange(blocks)[:, None, None]
    expert_ids = labels[block_index, position]
    return expert_ids.reshape(STEPS, TOKENS, TOP).astype(jnp.int32)


def draw_swap_pairs(key, part):
    shuffled = jax.random.permutation(jax.random.fold_in(key, 23), EXPERTS)
    return shuffled.reshape(PAIRS, 2).astype(jnp.int32)


def touch_ends(values, rng, least, high):
    index_at = [jax.random.randint(jax.random.fold_in(rng, axis), (), 0, length) for axis, length in enumerate(values.shape)]
    main_axis = values.shape.index(max(values.shape))
    next_to = index_at[:main_axis] + [(index_at[main_axis] + 1) % values.shape[main_axis]] + index_at[main_axis + 1:]
    return values.at[tuple(index_at)].set(least).at[tuple(next_to)].set(high)


def steps_of(rng, shape, pieces, least, high):
    gain = 1.0
    for dim, blocks in pieces:
        steps = jax.random.uniform(jax.random.fold_in(jax.random.fold_in(rng, 6), dim), (blocks,), jnp.float32, least / len(pieces), high / len(pieces))
        gain = gain * jnp.repeat(jnp.exp(steps), shape[dim] // blocks).reshape((-1,) + (1,) * (len(shape) - 1 - dim))
    return gain


def scatter_about(key, shape, deviation, limit, cuts=(), kind=jnp.bfloat16):
    array = jax.random.normal(key, shape, jnp.float32) * deviation
    if len(cuts) > 0:
        array = steps_of(key, shape, cuts, -0.22, 0.18) * array
    return jnp.clip(array, min=-limit, max=limit).astype(kind)


def setup_inputs(seed: int = 0) -> dict:
    splits = jax.random.split(jax.random.key(seed), 8)
    tokens = scatter_about(splits[0], (STEPS, TOKENS, D), 1.0, 6.0, ((1, 128),))
    routes = draw_routes(jax.random.fold_in(splits[7], 71), 0)
    gates = jnp.clip(jnp.exp(math.log(1.0) - 2.9957323 * jax.random.uniform(splits[2], (STEPS, TOKENS, TOP), jnp.float32) ** steps_of(splits[2], (STEPS, TOKENS, TOP), ((1, 128),), -0.2, 0.2)), 0.05, 1.0)
    gate_up = scatter_about(splits[3], (EXPERTS, D, 2 * F), D ** -0.5, 0.125, ((0, 32),))
    down = scatter_about(splits[4], (EXPERTS, D, F), F ** -0.5, 0.21875, ((0, 32),))
    expert_load = touch_ends(jax.random.randint(splits[5], (DOMAINS, EXPERTS), 1, 4096), jax.random.fold_in(splits[5], 1), 1, 4095).astype(jnp.int32)
    swap_pairs = draw_swap_pairs(jax.random.fold_in(splits[7], 71), 0)
    return {"tokens": tokens, "routes": routes, "gates": gates, "gate_up": gate_up, "down": down, "expert_load": expert_load, "swap_pairs": swap_pairs}


def slot_sources(swap_pairs):
    slots = jnp.arange(EXPERTS, dtype=jnp.int32)
    first = swap_pairs[:, 0:1]
    second = swap_pairs[:, 1:2]
    moves = jnp.where(first == slots[None, :], second - slots[None, :], 0)
    moves = moves + jnp.where(second == slots[None, :], first - slots[None, :], 0)
    return (slots + jnp.sum(moves, axis=0)).astype(jnp.int32)


def expert_rows(row_block, gate_up_one, down_one):
    gate_and_up = jnp.dot(row_block, gate_up_one, preferred_element_type=jnp.float32)
    hidden = (jax.nn.silu(gate_and_up[:, :F]) * gate_and_up[:, F:]).astype(jnp.bfloat16)
    result = lax.dot_general(hidden, down_one, (((1,), (1,)), ((), ())), preferred_element_type=jnp.float32)
    return result.astype(jnp.bfloat16)


def one_step(step_tokens, step_routes, step_gates, gate_up, down):
    flat_ids = step_routes.reshape(-1)
    weight = (step_gates / jnp.sum(step_gates, axis=1, keepdims=True)).reshape(-1)
    most_rows = (TOKENS // ROWS) * CAP

    def add_expert(expert_index, running):
        others = (flat_ids != expert_index).astype(jnp.int32)
        ordering = jnp.argsort(others, stable=True)[:most_rows].astype(jnp.int32)
        is_live = jnp.arange(most_rows, dtype=jnp.int32) < jnp.sum(1 - others)
        row_index = (ordering // TOP).astype(jnp.int32)
        picked = jnp.take(step_tokens, row_index, axis=0)
        gate_up_one = lax.dynamic_index_in_dim(gate_up, expert_index, 0, keepdims=False)
        down_one = lax.dynamic_index_in_dim(down, expert_index, 0, keepdims=False)
        result = expert_rows(picked, gate_up_one, down_one).astype(jnp.float32)
        scaling = jnp.where(is_live, jnp.take(weight, ordering), jnp.zeros((), weight.dtype))
        return running.at[row_index].add(result * scaling[:, None])

    start_total = jnp.zeros((TOKENS, D), jnp.float32)
    return lax.fori_loop(0, EXPERTS, add_expert, start_total)


def reference(tokens, routes, gates, gate_up, down, expert_load, swap_pairs):
    results = []
    for step_index in range(STEPS):
        results.append(one_step(tokens[step_index], routes[step_index], gates[step_index], gate_up, down))
    mixed = jnp.stack(results)
    sources = slot_sources(swap_pairs)
    moved_gate_up = jnp.take(gate_up, sources, axis=0)
    moved_down = jnp.take(down, sources, axis=0)
    total_load = jnp.sum(expert_load, axis=0)
    mean_load = jnp.sum(total_load).astype(jnp.float32) / EXPERTS
    slot_share = jnp.take(total_load, sources).astype(jnp.float32) / mean_load
    return (mixed, moved_gate_up, moved_down, slot_share)
```

```python
import functools

import jax
import jax.numpy as jnp
from jax import lax
from jax.experimental import pallas as pl
from jax.experimental.pallas import tpu as pltpu
from jax.sharding import PartitionSpec as P

MESH = pl.DeviceIdType.MESH
STEPS, ROWS, WIDE, HID, TOPK = 4, 16, 2048, 768, 8
HALF = WIDE // 2
QUART = HALF // 2
CHUNKS = ((0, 0), (0, 768), (1, 0))
CW = 768
K = len(CHUNKS)

PLAN = [
    (0, "W1", 0), (1, "side", 0), (2, "A1", 0), (3, "W1", 1), (4, "A1", 1), (4.1, "W0", 0),
    (6, "W2", 0), (7, "A2", 0), (8, "A1", 2), (8.1, "A1", 3), (8.2, "W1", 2),
    (9, "src", 0), (10, "W2", 1), (11, "W3", 0), (11.5, "A3", 0), (12, "A2", 1), (13, "W4", 0),
    (14, "W3", 1), (15, "A4", 0), (15.5, "A2", 2), (15.6, "A3", 1), (16, "A2", 3), (17, "wcol", 0),
    (18, "W4", 1), (19, "W5", 0), (20, "W2", 2), (20.5, "A5", 0), (21, "A4", 1), (21.5, "A3", 2),
    (24, "Y1", 0), (25, "W5", 1), (26, "A6", 0), (26.1, "A5", 1), (26.2, "W3", 2), (26.3, "A3", 3),
    (26.4, "A4", 2), (27, "C1", 0), (28, "W4", 2), (28.5, "Y1", 1), (28.6, "A5", 2), (28.7, "A4", 3),
    (29, "C2", 0), (29.5, "R1", 0), (29.6, "W5", 2), (29.7, "A6", 1), (30, "C1", 1), (30.2, "R2", 0),
    (30.3, "Y1", 2), (30.4, "A5", 3), (31, "C2", 1), (31.5, "R1", 1), (31.6, "R3", 0), (31.7, "A6", 2),
    (31.8, "Y2", 0), (32, "C1", 2), (32.1, "R2", 1), (32.2, "R4", 0), (33, "C2", 2), (33.1, "R1", 2),
    (33.2, "R3", 1), (33.3, "R5", 0), (33.4, "A6", 3), (34, "C1", 3), (34.1, "R2", 2), (34.2, "R4", 1),
    (35, "C2", 3), (35.1, "R1", 3), (35.2, "R3", 2), (35.3, "R5", 1), (35.4, "Y2", 1), (36, "R2", 3),
    (36.1, "R4", 2), (36.2, "R3", 3), (36.3, "R5", 2), (36.4, "R4", 3), (36.5, "R5", 3),
    (37, "Y2", 2), (38, "R6", 0), (38.1, "R6", 1), (38.2, "R6", 2), (38.3, "R6", 3),
    (39, "Y3", 0), (39.1, "Y3", 1), (39.2, "Y3", 2),
]


def kernel(
    tok, gu, dn, routes, gates, load, pairs,
    mixed, out_gu, out_dn, share,
    buf1, f0, f1, f2, f3, f4, f5, stage, buf3, xs, wgu, wdn, hid, part, sib, u0, t0, vv, t1, zz, u1, t2, v2, t3,
    wsend, wrecv, wcol, lsend, lrecv, srcs,
    rw, sw, ry, sy, ra, sa, rr, sr, misc,
):
    y = lax.axis_index("dp")
    e = lax.axis_index("expert")
    x, z, c = e // 8, (e // 2) % 4, e % 2

    def dev(dx=0, dz=0, dc=0, dy=0):
        return (
            lax.rem(y + dy, 4),
            (lax.rem(x + dx, 4) * 4 + lax.rem(z + dz, 4)) * 2 + lax.rem(c + dc, 2),
        )

    def first(h, o):
        return dev(dx=o) if h == 0 else dev(dz=o)

    def second(h, o):
        return dev(dz=o) if h == 0 else dev(dx=o)

    cf = (x, z)
    cg = (z, x)
    sends = []
    locals_ = []

    def remote(src, dst, ssem, rsem, device, own_send=True):
        cp = pltpu.make_async_remote_copy(
            src_ref=src, dst_ref=dst, send_sem=ssem, recv_sem=rsem, device_id=device, device_id_type=MESH
        )
        cp.start()
        if own_send:
            sends.append(cp)
        return cp

    def local(src, dst, sem):
        cp = pltpu.make_async_copy(src, dst, sem)
        cp.start()
        return cp

    def arrived(ref, sem):
        pltpu.make_async_copy(ref, ref, sem).wait()

    def shift(base, o):
        return lax.rem(base + o, 4)

    bar = pltpu.get_barrier_semaphore()

    def greet(k, carry):
        pl.semaphore_signal(bar, inc=1, device_id=(y, lax.rem(e + k, 32)), device_id_type=MESH)
        return carry

    lax.fori_loop(1, 32, greet, 0)
    for o in (1, 2, 3):
        pl.semaphore_signal(bar, inc=1, device_id=dev(dy=o), device_id_type=MESH)
    pl.semaphore_wait(bar, 34)

    weights = (gu, dn)
    full = ((f0, f1), (f2, f3), (f4, f5))
    moved = (out_gu, out_dn)

    def cols(k):
        return pl.ds(CHUNKS[k][1], CW)

    def region(k, h, yy):
        return moved[CHUNKS[k][0]].at[pl.ds(yy * 32 + h * 16, 16), :, cols(k)]

    def W0(_):
        local(gu, wgu, misc.at[0])
        local(dn, wdn, misc.at[1])

    def W1(k):
        for h in (0, 1):
            for o in (1, 3, 2, 0):
                i = shift(cf[h], o)
                src = weights[CHUNKS[k][0]].at[pl.ds(y * 32 + h * 16 + 4 * i, 4), :, cols(k)]
                dst = buf1.at[k, h, cf[h]]
                if o:
                    remote(src, dst, sw.at[k, h, 0], rw.at[k, h, 0], first(h, o), False)
                else:
                    local(src, dst, rw.at[k, h, 0])

    def W2(k):
        for h in (0, 1):
            arrived(buf1.at[k, h], rw.at[k, h, 0])
            for o in (1, 3, 2, 0):
                src = buf1.at[k, h, :, shift(cg[h], o)]
                dst = full[k][h].at[pl.ds(c * 16 + cg[h] * 4, 4)]
                if o:
                    remote(src, dst, sw.at[k, h, 1], rw.at[k, h, 1], second(h, o), False)
                else:
                    local(src, dst, rw.at[k, h, 1])

    def W3(k):
        for h in (0, 1):
            mine = full[k][h].at[pl.ds(c * 16, 16)]
            arrived(mine, rw.at[k, h, 1])
            remote(mine, mine, sw.at[k, h, 2], rw.at[k, h, 2], dev(dc=1))

    def src(_):
        def one(d, carry):
            slot = d * 2 + c
            total = jnp.int32(0)
            for i in range(16):
                a, b = pairs[i, 0], pairs[i, 1]
                total = total + jnp.where(a == slot, b, 0) + jnp.where(b == slot, a, 0)
            srcs[d] = total
            return carry

        lax.fori_loop(0, 16, one, 0)

    def W4(k):
        for h in (0, 1):
            arrived(full[k][h].at[pl.ds((1 - c) * 16, 16)], rw.at[k, h, 2])

            def pick(d, carry):
                s = srcs[d]
                sx, sz, sc = s // 8, (s // 2) % 4, s % 2
                dx, dz = d // 4, d % 4
                if h == 0:
                    stage[k, h, dz, dx] = full[k][h][sc * 16 + sz * 4 + sx]
                else:
                    stage[k, h, dx, dz] = full[k][h][sc * 16 + sx * 4 + sz]
                return carry

            lax.fori_loop(0, 16, pick, 0)
        for h in (0, 1):
            for o in (1, 3, 2, 0):
                src_ = stage.at[k, h, shift(cg[h], o)]
                dst = buf3.at[k, h, cg[h]]
                if o:
                    remote(src_, dst, sw.at[k, h, 3], rw.at[k, h, 3], second(h, o), False)
                else:
                    local(src_, dst, rw.at[k, h, 3])

    def W5(k):
        for h in (0, 1):
            arrived(buf3.at[k, h], rw.at[k, h, 3])
            for o in (1, 3, 2, 0):
                src_ = buf3.at[k, h, :, shift(cf[h], o)]
                dst = moved[CHUNKS[k][0]].at[pl.ds(y * 32 + h * 16 + 4 * cf[h], 4), :, cols(k)]
                if o:
                    remote(src_, dst, sw.at[k, h, 4], rw.at[k, h, 4], first(h, o), False)
                else:
                    local(src_, dst, rw.at[k, h, 4])

    def Y1(k):
        for h in (0, 1):
            mine = region(k, h, y)
            arrived(mine, rw.at[k, h, 4])
            remote(mine, mine, sy.at[k, h, 0], ry.at[k, h, 0], dev(dy=1))
            remote(mine, mine, sy.at[k, h, 1], ry.at[k, h, 1], dev(dy=3))

    def Y2(k):
        for h in (0, 1):
            below, above = shift(y, 3), shift(y, 1)
            arrived(region(k, h, below), ry.at[k, h, 0])
            part_ = region(k, h, below).at[pl.ds(0, 8)]
            remote(part_, part_, sy.at[k, h, 2], ry.at[k, h, 2], dev(dy=1))
            arrived(region(k, h, above), ry.at[k, h, 1])
            part_ = region(k, h, above).at[pl.ds(8, 8)]
            remote(part_, part_, sy.at[k, h, 3], ry.at[k, h, 3], dev(dy=3))

    def Y3(k):
        for h in (0, 1):
            far = region(k, h, shift(y, 2))
            arrived(far.at[pl.ds(0, 8)], ry.at[k, h, 2])
            arrived(far.at[pl.ds(8, 8)], ry.at[k, h, 3])

    def side(_):
        g = gates[...]
        w = g / jnp.sum(g, axis=1, keepdims=True)
        r = routes[...]
        lane = lax.broadcasted_iota(jnp.int32, (64, 128), 1)
        dense = jnp.zeros((64, 128), jnp.float32)
        for t in range(TOPK):
            dense = dense + jnp.where(r[:, t : t + 1] == lane, w[:, t : t + 1], 0.0)
        square = jnp.concatenate([dense, jnp.zeros((64, 128), jnp.float32)], axis=0)
        turned = jnp.transpose(square)
        for d in range(32):
            wsend[d] = jnp.broadcast_to(turned[d : d + 1], (8, 128))
        lsend[...] = jnp.zeros((8, 128), jnp.int32)
        lsend[0:2, 0:32] = load[...]
        for o in (1, 2, 3):
            remote(lsend, lrecv.at[y], misc.at[4 + o], misc.at[2], dev(dy=o))
        local(lsend, lrecv.at[y], misc.at[2])

        def give(k, carry):
            to = lax.rem(e + k, 32)
            remote(wsend.at[to], wrecv.at[e], misc.at[4], misc.at[3], (y, to), False)
            return carry

        lax.fori_loop(1, 32, give, 0)
        local(wsend.at[e], wrecv.at[e], misc.at[3])

    def wcol_(_):
        arrived(wrecv, misc.at[3])
        got = jnp.max(wrecv[...], axis=1)
        square = jnp.concatenate([got, jnp.zeros((96, 128), jnp.float32)], axis=0)
        wcol[...] = jnp.transpose(square)
        arrived(lrecv, misc.at[2])
        counts = jnp.sum(jnp.sum(lrecv[...], axis=0), axis=0, keepdims=True)
        lane = lax.broadcasted_iota(jnp.int32, (1, 128), 1)
        mine = jnp.int32(0)
        for i in range(16):
            a, b = pairs[i, 0], pairs[i, 1]
            mine = mine + jnp.where(a == e, b, 0) + jnp.where(b == e, a, 0)
        asf = counts.astype(jnp.float32)
        own = jnp.sum(jnp.where(lane == mine, asf, 0.0))
        share[0] = own / (jnp.sum(asf) / 32.0)

    def A1(s):
        for h in (0, 1):
            src_ = tok.at[s, :, pl.ds(h * HALF, HALF)]
            dst = xs.at[s, h, c, x, z]
            remote(src_, dst, sa.at[s, h, 0], ra.at[s, h, 0], first(h, 1))
            remote(src_, dst, sa.at[s, h, 1], ra.at[s, h, 1], first(h, 3))
            local(src_, dst, ra.at[s, h, 2])

    def at_f(s, h, i):
        return xs.at[s, h, c, i, z] if h == 0 else xs.at[s, h, c, x, i]

    def line(s, h, i):
        return xs.at[s, h, c, :, i] if h == 0 else xs.at[s, h, c, i]

    def A2(s):
        for h in (0, 1):
            lo, hi = at_f(s, h, shift(cf[h], 3)), at_f(s, h, shift(cf[h], 1))
            arrived(lo, ra.at[s, h, 0])
            lo = lo.at[:, pl.ds(0, QUART)]
            remote(lo, lo, sa.at[s, h, 3], ra.at[s, h, 3], first(h, 1))
            arrived(hi, ra.at[s, h, 1])
            hi = hi.at[:, pl.ds(QUART, QUART)]
            remote(hi, hi, sa.at[s, h, 4], ra.at[s, h, 4], first(h, 3))

    def A3(s):
        for h in (0, 1):
            far = at_f(s, h, shift(cf[h], 2))
            arrived(far.at[:, pl.ds(0, QUART)], ra.at[s, h, 3])
            arrived(far.at[:, pl.ds(QUART, QUART)], ra.at[s, h, 4])
            arrived(at_f(s, h, cf[h]), ra.at[s, h, 2])
            mine = line(s, h, cg[h])
            remote(mine, mine, sa.at[s, h, 5], ra.at[s, h, 5], second(h, 1))
            remote(mine, mine, sa.at[s, h, 6], ra.at[s, h, 6], second(h, 3))

    def A4(s):
        for h in (0, 1):
            lo, hi = line(s, h, shift(cg[h], 3)), line(s, h, shift(cg[h], 1))
            arrived(lo, ra.at[s, h, 5])
            lo = lo.at[:, :, pl.ds(0, QUART)]
            remote(lo, lo, sa.at[s, h, 7], ra.at[s, h, 7], second(h, 1))
            arrived(hi, ra.at[s, h, 6])
            hi = hi.at[:, :, pl.ds(QUART, QUART)]
            remote(hi, hi, sa.at[s, h, 8], ra.at[s, h, 8], second(h, 3))

    def A5(s):
        for h in (0, 1):
            far = line(s, h, shift(cg[h], 2))
            arrived(far.at[:, :, pl.ds(0, QUART)], ra.at[s, h, 7])
            arrived(far.at[:, :, pl.ds(QUART, QUART)], ra.at[s, h, 8])
            mine = xs.at[s, h, c]
            remote(mine, mine, sa.at[s, h, 9], ra.at[s, h, 9], dev(dc=1))

    def A6(s):
        if s == 0:
            arrived(wgu, misc.at[0])
            arrived(wdn, misc.at[1])
        for h in (0, 1):
            arrived(xs.at[s, h, 1 - c], ra.at[s, h, 9])

    def C1(s):
        def tile(n, carry):
            at = pl.multiple_of(n * 256, 256)
            g = jnp.zeros((512, 256), jnp.float32)
            u = jnp.zeros((512, 256), jnp.float32)
            for h in (0, 1):
                rows = xs[s, h].reshape(512, HALF)
                g = g + jnp.dot(
                    rows,
                    wgu[h * 64 : (h + 1) * 64, :, pl.ds(at, 256)].reshape(HALF, 256),
                    preferred_element_type=jnp.float32,
                )
                u = u + jnp.dot(
                    rows,
                    wgu[h * 64 : (h + 1) * 64, :, pl.ds(pl.multiple_of(at + HID, 256), 256)].reshape(HALF, 256),
                    preferred_element_type=jnp.float32,
                )
            hid[:, pl.ds(at, 256)] = (g / (1.0 + jnp.exp(-g)) * u).astype(jnp.bfloat16)
            return carry

        lax.fori_loop(0, 3, tile, 0)

    def C2(s):
        for h in (0, 1):

            def tile(j, carry):
                at = pl.multiple_of(j * QUART, QUART)
                o = lax.dot_general(
                    hid[...],
                    wdn[pl.ds(h * 64 + j * 32, 32)].reshape(QUART, HID),
                    (((1,), (1,)), ((), ())),
                    preferred_element_type=jnp.float32,
                )
                for cls in range(2):
                    for q in range(16):
                        d = cls * 16 + q
                        w = wcol[s * ROWS : (s + 1) * ROWS, q * 2 + cls : q * 2 + cls + 1]
                        piece = (o[d * ROWS : (d + 1) * ROWS] * w).astype(jnp.bfloat16)
                        part[s, h, cls, q // 4, q % 4, :, pl.ds(at, QUART)] = piece
                return carry

            lax.fori_loop(0, 2, tile, 0)

    def f32(v):
        return v.astype(jnp.float32)

    def b16(v):
        return v.astype(jnp.bfloat16)

    def chip(s, h, i):
        if h == 0:
            return f32(part[s, h, c, i]) + f32(sib[s, h, i])
        return f32(part[s, h, c, :, i]) + f32(sib[s, h, :, i])

    def R1(s):
        for h in (0, 1):
            remote(part.at[s, h, 1 - c], sib.at[s, h], sr.at[s, h, 0], rr.at[s, h, 0], dev(dc=1))

    LO, HI = pl.ds(0, QUART), pl.ds(QUART, QUART)

    def R2(s):
        for h in (0, 1):
            arrived(sib.at[s, h], rr.at[s, h, 0])
            u0[s, h] = b16(chip(s, h, shift(cf[h], 2)))
            remote(u0.at[s, h, :, :, LO], t0.at[s, h, :, :, LO], sr.at[s, h, 1], rr.at[s, h, 1], first(h, 1))
            remote(u0.at[s, h, :, :, HI], t0.at[s, h, :, :, HI], sr.at[s, h, 2], rr.at[s, h, 2], first(h, 3))

    def R3(s):
        for h in (0, 1):
            arrived(t0.at[s, h, :, :, LO], rr.at[s, h, 1])
            v = chip(s, h, shift(cf[h], 1))
            vv[s, h, 0, :, :, 0:QUART] = b16(v[:, :, 0:QUART] + f32(t0[s, h, :, :, 0:QUART]))
            vv[s, h, 0, :, :, QUART:HALF] = b16(v[:, :, QUART:HALF])
            remote(vv.at[s, h, 0], t1.at[s, h, 0], sr.at[s, h, 3], rr.at[s, h, 3], first(h, 1))
            arrived(t0.at[s, h, :, :, HI], rr.at[s, h, 2])
            v = chip(s, h, shift(cf[h], 3))
            vv[s, h, 1, :, :, 0:QUART] = b16(v[:, :, 0:QUART])
            vv[s, h, 1, :, :, QUART:HALF] = b16(v[:, :, QUART:HALF] + f32(t0[s, h, :, :, QUART:HALF]))
            remote(vv.at[s, h, 1], t1.at[s, h, 1], sr.at[s, h, 4], rr.at[s, h, 4], first(h, 3))

    def R4(s):
        for h in (0, 1):
            arrived(t1.at[s, h, 0], rr.at[s, h, 3])
            arrived(t1.at[s, h, 1], rr.at[s, h, 4])
            zz[s, h] = chip(s, h, cf[h]) + f32(t1[s, h, 0]) + f32(t1[s, h, 1])
            u1[s, h] = b16(zz[s, h, shift(cg[h], 2)])
            remote(u1.at[s, h, :, LO], t2.at[s, h, :, LO], sr.at[s, h, 5], rr.at[s, h, 5], second(h, 1))
            remote(u1.at[s, h, :, HI], t2.at[s, h, :, HI], sr.at[s, h, 6], rr.at[s, h, 6], second(h, 3))

    def R5(s):
        for h in (0, 1):
            arrived(t2.at[s, h, :, LO], rr.at[s, h, 5])
            v = zz[s, h, shift(cg[h], 1)]
            v2[s, h, 0, :, 0:QUART] = b16(v[:, 0:QUART] + f32(t2[s, h, :, 0:QUART]))
            v2[s, h, 0, :, QUART:HALF] = b16(v[:, QUART:HALF])
            remote(v2.at[s, h, 0], t3.at[s, h, 0], sr.at[s, h, 7], rr.at[s, h, 7], second(h, 1))
            arrived(t2.at[s, h, :, HI], rr.at[s, h, 6])
            v = zz[s, h, shift(cg[h], 3)]
            v2[s, h, 1, :, 0:QUART] = b16(v[:, 0:QUART])
            v2[s, h, 1, :, QUART:HALF] = b16(v[:, QUART:HALF] + f32(t2[s, h, :, QUART:HALF]))
            remote(v2.at[s, h, 1], t3.at[s, h, 1], sr.at[s, h, 8], rr.at[s, h, 8], second(h, 3))

    def R6(s):
        for h in (0, 1):
            arrived(t3.at[s, h, 0], rr.at[s, h, 7])
            arrived(t3.at[s, h, 1], rr.at[s, h, 8])
            mixed[s, :, h * HALF : (h + 1) * HALF] = zz[s, h, cg[h]] + f32(t3[s, h, 0]) + f32(t3[s, h, 1])

    tasks = dict(
        W0=W0, W1=W1, W2=W2, W3=W3, W4=W4, W5=W5, Y1=Y1, Y2=Y2, Y3=Y3, src=src, side=side, wcol=wcol_,
        A1=A1, A2=A2, A3=A3, A4=A4, A5=A5, A6=A6, C1=C1, C2=C2, R1=R1, R2=R2, R3=R3, R4=R4, R5=R5, R6=R6,
    )
    for _, name, index in sorted(PLAN, key=lambda p: p[0]):
        tasks[name](index)

    for cp in sends:
        cp.wait_send()
    for k in range(K):
        for h in (0, 1):
            for step in (0, 1, 3, 4):
                arrived(buf3.at[k, h, pl.ds(0, 3)], sw.at[k, h, step])
    arrived(wsend.at[pl.ds(0, 31)], misc.at[4])


def on_device(tokens, routes, gates, gate_up, down, expert_load, swap_pairs):
    hbm = pl.BlockSpec(memory_space=pltpu.HBM)
    vmem = pl.BlockSpec(memory_space=pltpu.VMEM)
    smem = pl.BlockSpec(memory_space=pltpu.SMEM)
    bf, f = jnp.bfloat16, jnp.float32
    sem = pltpu.SemaphoreType.DMA
    mixed, gu, dn, share = pl.pallas_call(
        kernel,
        out_shape=(
            jax.ShapeDtypeStruct((STEPS, ROWS, WIDE), f),
            jax.ShapeDtypeStruct((128, 16, 2 * HID), bf),
            jax.ShapeDtypeStruct((128, 16, HID), bf),
            jax.ShapeDtypeStruct((1,), f),
        ),
        in_specs=[hbm, hbm, hbm, vmem, vmem, vmem, smem],
        out_specs=(vmem, hbm, hbm, smem),
        scratch_shapes=[
            pltpu.VMEM((K, 2, 4, 4, 16, CW), bf),
            *[pltpu.VMEM((32, 16, CW), bf)] * (2 * K),
            pltpu.VMEM((K, 2, 4, 4, 16, CW), bf),
            pltpu.VMEM((K, 2, 4, 4, 16, CW), bf),
            pltpu.VMEM((STEPS, 2, 2, 4, 4, ROWS, HALF), bf),
            pltpu.VMEM((128, 16, 2 * HID), bf),
            pltpu.VMEM((128, 16, HID), bf),
            pltpu.VMEM((512, HID), bf),
            pltpu.VMEM((STEPS, 2, 2, 4, 4, ROWS, HALF), bf),
            pltpu.VMEM((STEPS, 2, 4, 4, ROWS, HALF), bf),
            pltpu.VMEM((STEPS, 2, 4, ROWS, HALF), bf),
            pltpu.VMEM((STEPS, 2, 4, ROWS, HALF), bf),
            pltpu.VMEM((STEPS, 2, 2, 4, ROWS, HALF), bf),
            pltpu.VMEM((STEPS, 2, 2, 4, ROWS, HALF), bf),
            pltpu.VMEM((STEPS, 2, 4, ROWS, HALF), f),
            pltpu.VMEM((STEPS, 2, ROWS, HALF), bf),
            pltpu.VMEM((STEPS, 2, ROWS, HALF), bf),
            pltpu.VMEM((STEPS, 2, 2, ROWS, HALF), bf),
            pltpu.VMEM((STEPS, 2, 2, ROWS, HALF), bf),
            pltpu.VMEM((32, 8, 128), f),
            pltpu.VMEM((32, 8, 128), f),
            pltpu.VMEM((128, 128), f),
            pltpu.VMEM((8, 128), jnp.int32),
            pltpu.VMEM((4, 8, 128), jnp.int32),
            pltpu.SMEM((16,), jnp.int32),
            sem((K, 2, 5)),
            sem((K, 2, 5)),
            sem((K, 2, 4)),
            sem((K, 2, 4)),
            sem((STEPS, 2, 10)),
            sem((STEPS, 2, 10)),
            sem((STEPS, 2, 9)),
            sem((STEPS, 2, 9)),
            sem((8,)),
        ],
        compiler_params=pltpu.CompilerParams(
            collective_id=0, has_side_effects=True, vmem_limit_bytes=62 * 1024 * 1024
        ),
    )(
        tokens,
        gate_up.reshape(128, 16, 2 * HID),
        down.reshape(128, 16, HID),
        routes.reshape(STEPS * ROWS, TOPK),
        gates.reshape(STEPS * ROWS, TOPK),
        expert_load,
        swap_pairs,
    )
    return mixed, gu.reshape(1, WIDE, 2 * HID), dn.reshape(1, WIDE, HID), share


def solution(mesh):
    placed = (
        P(None, ("dp", "expert"), None),
        P(None, ("dp", "expert"), None),
        P(None, ("dp", "expert"), None),
        P("expert", None, None),
        P("expert", None, None),
        P("dp", None),
        P(),
    )
    return jax.shard_map(
        on_device,
        mesh=mesh,
        in_specs=placed,
        out_specs=(
            P(None, ("dp", "expert"), None),
            P("expert", None, None),
            P("expert", None, None),
            P("expert"),
        ),
        check_vma=False,
    )
```

```python
import math

import jax
import jax.numpy as jnp
from jax import lax
from jax.experimental import pallas as pl
from jax.experimental.pallas import tpu as pltpu
from jax.sharding import PartitionSpec as P

MESH = pl.DeviceIdType.MESH
STEPS, ROWS, WIDE, HID, TOPK = 4, 16, 2048, 768, 8
HALF = WIDE // 2
QUART = HALF // 2
CW = 384
CHUNKS = [(0, at) for at in range(0, 2 * HID, CW)] + [(1, at) for at in range(0, HID, CW)]
K = len(CHUNKS)
HB = 2

(
    W1, W2, W3, W4, W5, Y1, Y2, Y3, A1, A2, A3, A4, A5, C1, C2, R2, R3, R4, R5, R6, SR, WA, WB, WC, WD,
) = range(25)
X, Z = 0, 1
PLAN = [
    (W1, 3, Z), (A1, 0, X), (W1, 4, X), (W1, 2, X), (A1, 0, Z), (SR, 0, X), (W1, 4, Z), (A2, 0, X), (W1, 2, Z),
    (W2, 3, Z), (W1, 0, X), (A2, 0, Z), (W2, 4, X), (W2, 2, X), (A3, 0, X), (A1, 1, X), (A3, 0, Z), (W3, 3, Z),
    (WA, 0, X), (W3, 4, X), (W4, 3, Z), (W2, 2, Z), (W2, 0, X), (W3, 2, X), (W1, 3, X), (A4, 0, Z), (W4, 4, X),
    (W5, 3, Z), (A2, 1, X), (WB, 0, X), (A1, 1, Z), (A1, 3, X), (W4, 2, X), (W5, 4, X), (W2, 4, Z), (A1, 2, X),
    (W3, 0, X), (A4, 0, X), (A1, 2, Z), (Y1, 3, Z), (W3, 2, Z), (A5, 0, Z), (A2, 1, Z), (W4, 0, X), (W2, 3, X),
    (A3, 1, X), (W5, 2, X), (WC, 0, X), (A2, 3, X), (Y1, 4, X), (A3, 1, Z), (A5, 0, X), (W4, 2, Z), (A1, 3, Z),
    (W1, 0, Z), (W3, 4, Z), (W1, 1, Z), (A2, 2, X), (Y2, 3, Z), (WD, 0, X), (A2, 2, Z), (Y1, 2, X), (W5, 0, X),
    (C1, 0, X), (A4, 1, Z), (W4, 4, Z), (Y2, 4, X), (A4, 1, X), (W5, 2, Z), (C2, 0, X), (W3, 3, X), (W2, 0, Z),
    (A3, 2, X), (Y1, 0, X), (Y2, 2, X), (A5, 1, Z), (A3, 2, Z), (A5, 1, X), (W1, 1, X), (C2, 0, Z), (W2, 1, Z),
    (W5, 4, Z), (W1, 5, X), (W4, 3, X), (Y1, 2, Z), (W1, 5, Z), (A2, 3, Z), (W3, 0, Z), (C1, 1, X), (A4, 2, X),
    (Y1, 4, Z), (W2, 1, X), (A4, 2, Z), (W4, 0, Z), (A3, 3, X), (C2, 1, X), (W5, 3, X), (R2, 0, Z), (Y2, 0, X),
    (W2, 5, Z), (Y2, 2, Z), (W3, 1, Z), (A3, 3, Z), (A5, 2, Z), (A5, 2, X), (C2, 1, Z), (W4, 1, Z), (R2, 0, X),
    (W5, 0, Z), (R2, 1, X), (Y2, 4, Z), (W2, 5, X), (W3, 1, X), (A4, 3, X), (Y1, 3, X), (C1, 2, X), (W4, 1, X),
    (W3, 5, Z), (Y1, 0, Z), (C2, 2, X), (R2, 1, Z), (A4, 3, Z), (W5, 1, Z), (W3, 5, X), (W4, 5, Z), (Y2, 3, X),
    (A5, 3, X), (C2, 2, Z), (R2, 2, X), (R3, 0, Z), (A5, 3, Z), (W5, 1, X), (R3, 1, X), (Y2, 0, Z), (W4, 5, X),
    (R2, 2, Z), (Y1, 1, Z), (R3, 0, X), (W5, 5, Z), (C1, 3, X), (Y1, 1, X), (C2, 3, X), (W5, 5, X), (C2, 3, Z),
    (Y2, 1, Z), (R3, 2, Z), (R2, 3, X), (Y1, 5, Z), (R3, 2, X), (R2, 3, Z), (R4, 0, Z), (R3, 1, Z), (Y3, 4, X),
    (Y3, 2, X), (R3, 3, X), (Y1, 5, X), (R4, 2, Z), (Y2, 1, X), (R3, 3, Z), (Y3, 1, Z), (Y3, 3, X), (R4, 2, X),
    (R4, 1, X), (R4, 1, Z), (Y2, 5, Z), (R4, 0, X), (R5, 2, Z), (R4, 3, X), (R5, 0, Z), (R4, 3, Z), (R5, 2, X),
    (Y3, 2, Z), (R5, 1, Z), (R5, 0, X), (R5, 1, X), (Y2, 5, X), (R5, 3, X), (Y3, 4, Z), (R6, 0, Z), (R5, 3, Z),
    (Y3, 0, Z), (Y3, 1, X), (R6, 2, X), (R6, 2, Z), (R6, 1, Z), (Y3, 5, Z), (R6, 0, X), (Y3, 3, Z), (Y3, 0, X),
    (R6, 1, X), (R6, 3, X), (R6, 3, Z), (Y3, 5, X),
]

STAGES = [
    "W1", "W2", "W3", "W4", "W5", "Y1+", "Y1-", "Y2+", "Y2-",
    "A1+", "A1-", "A2+", "A2-", "A3+", "A3-", "A4+", "A4-", "A5",
    "R1", "R2+", "R2-", "R3+", "R3-", "R4+", "R4-", "R5+", "R5-",
    "WA", "WB", "WC", "L1", "L2", "L3",
]
AT = {name: i for i, name in enumerate(STAGES)}


def kernel(
    tok, gu, dn, routes_in, gates_in, load_in, pairs, mixed, out_gu, out_dn, share, *rest,
):
    full = [rest[2 * k : 2 * k + 2] for k in range(K)]
    (
        buf1, stage, buf3, xs, wgu, wdn, hid, part, sib, t0, t1, zz, u1, t2, v2, t3,
        routes, gates, load, wflat, wsend, wb1, wb2, wb3, wcol, lsend, lrecv, srcs, ss, rw, ry, ra, rr, misc,
    ) = rest[2 * K :]
    y = lax.axis_index("dp")
    e = lax.axis_index("expert")
    x, z, c = e // 8, (e // 2) % 4, e % 2

    def dev(dx=0, dz=0, dc=0, dy=0):
        return (
            lax.rem(y + dy, 4),
            (lax.rem(x + dx, 4) * 4 + lax.rem(z + dz, 4)) * 2 + lax.rem(c + dc, 2),
        )

    def first(h, o):
        return dev(dx=o) if h == 0 else dev(dz=o)

    def second(h, o):
        return dev(dz=o) if h == 0 else dev(dx=o)

    cf = (x, z)
    cg = (z, x)
    sent = {}

    def remote(name, src, dst, rsem, device):
        sent[name] = sent.get(name, 0) + math.prod(src.shape) * 2
        pltpu.make_async_remote_copy(
            src_ref=src, dst_ref=dst, send_sem=ss.at[AT[name]], recv_sem=rsem,
            device_id=device, device_id_type=MESH,
        ).start()

    def local(src, dst, sem):
        pltpu.make_async_copy(src, dst, sem).start()

    def arrived(ref, sem):
        pltpu.make_async_copy(ref, ref, sem).wait()

    def shift(base, o):
        return lax.rem(base + o, 4)

    weights = (gu, dn)
    moved = (out_gu, out_dn)

    def cols(k):
        return pl.ds(CHUNKS[k][1], CW)

    def region(k, h, yy):
        return moved[CHUNKS[k][0]].at[pl.ds(yy * 32 + h * 16, 16), :, cols(k)]

    def W1(k, h):
        for o in (1, 3, 2, 0):
            i = shift(cf[h], o)
            src = weights[CHUNKS[k][0]].at[pl.ds(y * 32 + h * 16 + 4 * i, 4), :, cols(k)]
            dst = buf1.at[k, h, cf[h]]
            if o:
                remote("W1", src, dst, rw.at[k, h, 0], first(h, o))
            else:
                local(src, dst, rw.at[k, h, 0])

    def W2(k, h):
        arrived(buf1.at[k, h], rw.at[k, h, 0])
        for o in (1, 3, 2, 0):
            src = buf1.at[k, h, :, shift(cg[h], o)]
            dst = full[k][h].at[pl.ds(c * 16 + cg[h] * 4, 4)]
            if o:
                remote("W2", src, dst, rw.at[k, h, 1], second(h, o))
            else:
                local(src, dst, rw.at[k, h, 1])

    def W3(k, h):
        mine = full[k][h].at[pl.ds(c * 16, 16)]
        arrived(mine, rw.at[k, h, 1])
        remote("W3", mine, mine, rw.at[k, h, 2], dev(dc=1))

    def W4(k, h):
        arrived(full[k][h].at[pl.ds((1 - c) * 16, 16)], rw.at[k, h, 2])
        for d in range(16):
            s = srcs[d]
            sx, sz, sc = s // 8, (s // 2) % 4, s % 2
            dx, dz = d // 4, d % 4
            if h == 0:
                stage[k, h, dz, dx] = full[k][h][sc * 16 + sz * 4 + sx]
            else:
                stage[k, h, dx, dz] = full[k][h][sc * 16 + sx * 4 + sz]
        for o in (1, 3, 2, 0):
            src = stage.at[k, h, shift(cg[h], o)]
            dst = buf3.at[k, h, cg[h]]
            if o:
                remote("W4", src, dst, rw.at[k, h, 3], second(h, o))
            else:
                local(src, dst, rw.at[k, h, 3])

    def W5(k, h):
        arrived(buf3.at[k, h], rw.at[k, h, 3])
        for o in (1, 3, 2, 0):
            src = buf3.at[k, h, :, shift(cf[h], o)]
            dst = moved[CHUNKS[k][0]].at[pl.ds(y * 32 + h * 16 + 4 * cf[h], 4), :, cols(k)]
            if o:
                remote("W5", src, dst, rw.at[k, h, 4], first(h, o))
            else:
                local(src, dst, rw.at[k, h, 4])

    def Y1(k, h):
        mine = region(k, h, y)
        arrived(mine, rw.at[k, h, 4])
        remote("Y1+", mine, mine, ry.at[k, h, 0], dev(dy=1))
        remote("Y1-", mine, mine, ry.at[k, h, 0], dev(dy=3))

    def Y2(k, h):
        arrived(buf1.at[pl.ds(0, 2), 0], ry.at[k, h, 0])
        up = region(k, h, shift(y, 3)).at[pl.ds(0, 8)]
        remote("Y2+", up, up, ry.at[k, h, 1], dev(dy=1))
        down = region(k, h, shift(y, 1)).at[pl.ds(8, 8)]
        remote("Y2-", down, down, ry.at[k, h, 1], dev(dy=3))

    def Y3(k, h):
        arrived(region(k, h, shift(y, 2)), ry.at[k, h, 1])

    def SR(_, __):
        def one(d, carry):
            slot = d * 2 + c
            total = jnp.int32(0)
            for i in range(16):
                a, b = pairs[0, i], pairs[1, i]
                total = total + jnp.where(a == slot, b, 0) + jnp.where(b == slot, a, 0)
            srcs[d] = total
            return carry

        lax.fori_loop(0, 16, one, 0)

    def side():
        arrived(routes, misc.at[6])
        arrived(gates, misc.at[7])
        arrived(load, misc.at[8])
        expert = lax.broadcasted_iota(jnp.int32, (32, ROWS), 0)
        for s in range(STEPS):
            g = gates[s]
            w = g / jnp.sum(g, axis=0, keepdims=True)
            r = routes[s]
            dense = jnp.zeros((32, ROWS), jnp.float32)
            for t in range(TOPK):
                dense = dense + jnp.where(r[t : t + 1] == expert, w[t : t + 1], 0.0)
            wflat[0:32, s * ROWS : (s + 1) * ROWS] = dense
        for d in range(32):
            wsend[d // 8, (d // 2) % 4, d % 2] = wflat[d : d + 1]
        lsend[...] = jnp.zeros((8, 128), jnp.int32)
        lsend[0:2, 0:32] = load[...]

    def WA(_, __):
        side()
        for o in (1, 3, 2):
            remote("WA", wsend.at[shift(x, o)], wb1.at[x], misc.at[0], dev(dx=o))
        local(wsend.at[x], wb1.at[x], misc.at[0])
        for o in (1, 2, 3):
            remote("L%d" % o, lsend, lrecv.at[y], misc.at[3], dev(dy=o))
        local(lsend, lrecv.at[y], misc.at[3])

    def WB(_, __):
        arrived(wb1, misc.at[0])
        for o in (1, 3, 2):
            remote("WB", wb1.at[:, shift(z, o)], wb2.at[:, z], misc.at[1], dev(dz=o))
        local(wb1.at[:, z], wb2.at[:, z], misc.at[1])

    def WC(_, __):
        arrived(wb2, misc.at[1])
        remote("WC", wb2.at[:, :, 1 - c], wb3.at[c], misc.at[2], dev(dc=1))
        local(wb2.at[:, :, c], wb3.at[c], misc.at[2])

    def WD(_, __):
        arrived(wb3, misc.at[2])
        wflat[...] = jnp.zeros((128, 128), jnp.float32)
        for d in range(32):
            wflat[d : d + 1] = wb3[d // 16, (d // 4) % 4, d % 4]
        wcol[...] = jnp.transpose(wflat[...])
        arrived(lrecv, misc.at[3])
        counts = jnp.sum(jnp.sum(lrecv[...], axis=0), axis=0, keepdims=True)
        lane = lax.broadcasted_iota(jnp.int32, (1, 128), 1)
        mine = jnp.int32(0)
        for i in range(16):
            a, b = pairs[0, i], pairs[1, i]
            mine = mine + jnp.where(a == e, b, 0) + jnp.where(b == e, a, 0)
        asf = counts.astype(jnp.float32)
        own = jnp.sum(jnp.where(lane == mine, asf, 0.0))
        share[0] = own / (jnp.sum(asf) / 32.0)

    def at_f(s, h, i):
        return xs.at[s, h, c, i, z] if h == 0 else xs.at[s, h, c, x, i]

    def line(s, h, i):
        return xs.at[s, h, c, :, i] if h == 0 else xs.at[s, h, c, i]

    LO, HI = pl.ds(0, QUART), pl.ds(QUART, QUART)

    def A1(s, h):
        src = tok.at[s, :, pl.ds(h * HALF, HALF)]
        dst = xs.at[s, h, c, x, z]
        remote("A1+", src, dst, ra.at[s, h, 0], first(h, 1))
        remote("A1-", src, dst, ra.at[s, h, 0], first(h, 3))
        local(src, dst, ra.at[s, h, 0])

    def A2(s, h):
        arrived(xs.at[s, h, 0, 0, pl.ds(0, 3)], ra.at[s, h, 0])
        lo = at_f(s, h, shift(cf[h], 3)).at[:, LO]
        remote("A2+", lo, lo, ra.at[s, h, 1], first(h, 1))
        hi = at_f(s, h, shift(cf[h], 1)).at[:, HI]
        remote("A2-", hi, hi, ra.at[s, h, 1], first(h, 3))

    def A3(s, h):
        arrived(at_f(s, h, shift(cf[h], 2)), ra.at[s, h, 1])
        mine = line(s, h, cg[h])
        remote("A3+", mine, mine, ra.at[s, h, 2], second(h, 1))
        remote("A3-", mine, mine, ra.at[s, h, 2], second(h, 3))

    def A4(s, h):
        arrived(xs.at[s, h, 0, pl.ds(0, 2)], ra.at[s, h, 2])
        lo = line(s, h, shift(cg[h], 3)).at[:, :, LO]
        remote("A4+", lo, lo, ra.at[s, h, 3], second(h, 1))
        hi = line(s, h, shift(cg[h], 1)).at[:, :, HI]
        remote("A4-", hi, hi, ra.at[s, h, 3], second(h, 3))

    def A5(s, h):
        arrived(line(s, h, shift(cg[h], 2)), ra.at[s, h, 3])
        mine = xs.at[s, h, c]
        remote("A5", mine, mine, ra.at[s, h, 4], dev(dc=1))

    loaded = []

    def C1(s, _):
        if not loaded:
            loaded.append(1)
            arrived(wgu, misc.at[4])
            arrived(wdn, misc.at[5])
        for h in (0, 1):
            arrived(xs.at[s, h, 1 - c], ra.at[s, h, 4])

        def tile(n, carry):
            at = pl.multiple_of(n * 256, 256)
            g = jnp.zeros((512, 256), jnp.float32)
            u = jnp.zeros((512, 256), jnp.float32)
            for h in (0, 1):
                rows = xs[s, h].reshape(512, HALF)
                g = g + jnp.dot(
                    rows,
                    wgu[h * 64 : (h + 1) * 64, :, pl.ds(at, 256)].reshape(HALF, 256),
                    preferred_element_type=jnp.float32,
                )
                u = u + jnp.dot(
                    rows,
                    wgu[h * 64 : (h + 1) * 64, :, pl.ds(pl.multiple_of(at + HID, 256), 256)].reshape(HALF, 256),
                    preferred_element_type=jnp.float32,
                )
            hid[s % HB, :, pl.ds(at, 256)] = (g / (1.0 + jnp.exp(-g)) * u).astype(jnp.bfloat16)
            return carry

        lax.fori_loop(0, 3, tile, 0)

    def C2(s, h):
        def tile(j, carry):
            at = pl.multiple_of(j * QUART, QUART)
            o = lax.dot_general(
                hid[s % HB],
                wdn[pl.ds(h * 64 + j * 32, 32)].reshape(QUART, HID),
                (((1,), (1,)), ((), ())),
                preferred_element_type=jnp.float32,
            )
            for d in range(32):
                w = wcol[s * ROWS : (s + 1) * ROWS, d : d + 1]
                piece = (o[d * ROWS : (d + 1) * ROWS] * w).astype(jnp.bfloat16)
                part[s, h, d // 16, (d // 4) % 4, d % 4, :, pl.ds(at, QUART)] = piece
            return carry

        lax.fori_loop(0, 2, tile, 0)
        remote("R1", part.at[s, h, 1 - c], sib.at[s, h], rr.at[s, h, 0], dev(dc=1))

    def f32(v):
        return v.astype(jnp.float32)

    def b16(v):
        return v.astype(jnp.bfloat16)

    def chip(s, h, i):
        if h == 0:
            return f32(part[s, h, c, i]) + f32(sib[s, h, i])
        return f32(part[s, h, c, :, i]) + f32(sib[s, h, :, i])

    def mine(s, h, i):
        return part.at[s, h, c, i] if h == 0 else part.at[s, h, c, :, i]

    def keep(s, h, i, cut, value):
        if h == 0:
            part[s, h, c, i, :, :, cut] = b16(value)
        else:
            part[s, h, c, :, i, :, cut] = b16(value)

    def R2(s, h):
        arrived(sib.at[s, h], rr.at[s, h, 0])
        i = shift(cf[h], 2)
        keep(s, h, i, slice(0, HALF), chip(s, h, i))
        remote("R2+", mine(s, h, i).at[:, :, LO], t0.at[s, h, :, :, LO], rr.at[s, h, 1], first(h, 1))
        remote("R2-", mine(s, h, i).at[:, :, HI], t0.at[s, h, :, :, HI], rr.at[s, h, 1], first(h, 3))

    def R3(s, h):
        arrived(t0.at[s, h], rr.at[s, h, 1])
        i = shift(cf[h], 1)
        v = chip(s, h, i)
        keep(s, h, i, slice(0, QUART), v[:, :, 0:QUART] + f32(t0[s, h, :, :, 0:QUART]))
        keep(s, h, i, slice(QUART, HALF), v[:, :, QUART:HALF])
        remote("R3+", mine(s, h, i), t1.at[s, h, 0], rr.at[s, h, 2], first(h, 1))
        i = shift(cf[h], 3)
        v = chip(s, h, i)
        keep(s, h, i, slice(0, QUART), v[:, :, 0:QUART])
        keep(s, h, i, slice(QUART, HALF), v[:, :, QUART:HALF] + f32(t0[s, h, :, :, QUART:HALF]))
        remote("R3-", mine(s, h, i), t1.at[s, h, 1], rr.at[s, h, 2], first(h, 3))

    def R4(s, h):
        arrived(t1.at[s, h], rr.at[s, h, 2])
        zz[s, h] = chip(s, h, cf[h]) + f32(t1[s, h, 0]) + f32(t1[s, h, 1])
        u1[s, h] = b16(zz[s, h, shift(cg[h], 2)])
        remote("R4+", u1.at[s, h, :, LO], t2.at[s, h, :, LO], rr.at[s, h, 3], second(h, 1))
        remote("R4-", u1.at[s, h, :, HI], t2.at[s, h, :, HI], rr.at[s, h, 3], second(h, 3))

    def R5(s, h):
        arrived(t2.at[s, h], rr.at[s, h, 3])
        v = zz[s, h, shift(cg[h], 1)]
        v2[s, h, 0, :, 0:QUART] = b16(v[:, 0:QUART] + f32(t2[s, h, :, 0:QUART]))
        v2[s, h, 0, :, QUART:HALF] = b16(v[:, QUART:HALF])
        remote("R5+", v2.at[s, h, 0], t3.at[s, h, 0], rr.at[s, h, 4], second(h, 1))
        v = zz[s, h, shift(cg[h], 3)]
        v2[s, h, 1, :, 0:QUART] = b16(v[:, 0:QUART])
        v2[s, h, 1, :, QUART:HALF] = b16(v[:, QUART:HALF] + f32(t2[s, h, :, QUART:HALF]))
        remote("R5-", v2.at[s, h, 1], t3.at[s, h, 1], rr.at[s, h, 4], second(h, 3))

    def R6(s, h):
        arrived(t3.at[s, h], rr.at[s, h, 4])
        mixed[s, :, h * HALF : (h + 1) * HALF] = zz[s, h, cg[h]] + f32(t3[s, h, 0]) + f32(t3[s, h, 1])

    bar = pltpu.get_barrier_semaphore()
    peers = [dev(dc=1)]
    for o in (1, 2, 3):
        peers += [dev(dx=o), dev(dz=o), dev(dy=o)]
    for peer in peers:
        pl.semaphore_signal(bar, inc=1, device_id=peer, device_id_type=MESH)
    for n, (src, dst) in enumerate(((routes_in, routes), (gates_in, gates), (load_in, load))):
        local(src, dst, misc.at[6 + n])
    pl.semaphore_wait(bar, len(peers))

    tasks = (
        W1, W2, W3, W4, W5, Y1, Y2, Y3, A1, A2, A3, A4, A5, C1, C2, R2, R3, R4, R5, R6, SR, WA, WB, WC, WD,
    )
    for number, item in enumerate(PLAN):
        stage_of, index, half = item
        tasks[stage_of](index, half)
        if number == 8:
            local(gu, wgu, misc.at[4])
            local(dn, wdn, misc.at[5])

    total = dict(
        {name: buf1.at[:, :, pl.ds(0, 3)] for name in ("W1", "W2", "W4", "W5")},
        **{name: buf1 for name in ("W3", "Y1+", "Y1-")},
        **{name: buf1.at[:, 0] for name in ("Y2+", "Y2-")},
        **{name: u1 for name in ("A1+", "A1-")},
        **{name: u1.at[:, :, :, LO] for name in ("A2+", "A2-", "R4+", "R4-")},
        **{name: t0 for name in ("A3+", "A3-", "R3+", "R3-")},
        **{name: t0.at[:, :, :, :, LO] for name in ("A4+", "A4-", "R2+", "R2-")},
        **{name: sib for name in ("A5", "R1")},
        **{name: u1 for name in ("R5+", "R5-")},
        WA=wsend.at[pl.ds(0, 3)], WB=wb1.at[:, pl.ds(0, 3)], WC=wb3.at[0],
        L1=lsend, L2=lsend, L3=lsend,
    )
    for name in sent:
        assert math.prod(total[name].shape) * 2 == sent[name], name
        arrived(total[name], ss.at[AT[name]])


def on_device(tokens, routes, gates, gate_up, down, expert_load, swap_pairs):
    hbm = pl.BlockSpec(memory_space=pltpu.HBM)
    vmem = pl.BlockSpec(memory_space=pltpu.VMEM)
    smem = pl.BlockSpec(memory_space=pltpu.SMEM)
    bf, f = jnp.bfloat16, jnp.float32
    sem = pltpu.SemaphoreType.DMA
    shapes = (
        jax.ShapeDtypeStruct((STEPS, ROWS, WIDE), f),
        jax.ShapeDtypeStruct((128, 16, 2 * HID), bf),
        jax.ShapeDtypeStruct((128, 16, HID), bf),
        jax.ShapeDtypeStruct((1,), f),
    )
    mixed, gu, dn, share = pl.pallas_call(
        kernel,
        out_shape=(pltpu.VMEM(shapes[0].shape, f), pltpu.VMEM(shapes[1].shape, bf), pltpu.VMEM(shapes[2].shape, bf), shapes[3]),
        in_specs=[hbm, hbm, hbm, hbm, hbm, hbm, smem],
        out_specs=(vmem, vmem, vmem, smem),
        scratch_shapes=[
            *[pltpu.VMEM((32, 16, CW), bf)] * (2 * K),
            pltpu.VMEM((K, 2, 4, 4, 16, CW), bf),
            pltpu.VMEM((K, 2, 4, 4, 16, CW), bf),
            pltpu.VMEM((K, 2, 4, 4, 16, CW), bf),
            pltpu.VMEM((STEPS, 2, 2, 4, 4, ROWS, HALF), bf),
            pltpu.VMEM((128, 16, 2 * HID), bf),
            pltpu.VMEM((128, 16, HID), bf),
            pltpu.VMEM((HB, 512, HID), bf),
            pltpu.VMEM((STEPS, 2, 2, 4, 4, ROWS, HALF), bf),
            pltpu.VMEM((STEPS, 2, 4, 4, ROWS, HALF), bf),
            pltpu.VMEM((STEPS, 2, 4, ROWS, HALF), bf),
            pltpu.VMEM((STEPS, 2, 2, 4, ROWS, HALF), bf),
            pltpu.VMEM((STEPS, 2, 4, ROWS, HALF), f),
            pltpu.VMEM((STEPS, 2, ROWS, HALF), bf),
            pltpu.VMEM((STEPS, 2, ROWS, HALF), bf),
            pltpu.VMEM((STEPS, 2, 2, ROWS, HALF), bf),
            pltpu.VMEM((STEPS, 2, 2, ROWS, HALF), bf),
            pltpu.VMEM((STEPS, TOPK, ROWS), jnp.int32),
            pltpu.VMEM((STEPS, TOPK, ROWS), f),
            pltpu.VMEM((2, 32), jnp.int32),
            pltpu.VMEM((128, 128), f),
            pltpu.VMEM((4, 4, 2, 1, 128), f),
            pltpu.VMEM((4, 4, 2, 1, 128), f),
            pltpu.VMEM((4, 4, 2, 1, 128), f),
            pltpu.VMEM((2, 4, 4, 1, 128), f),
            pltpu.VMEM((128, 128), f),
            pltpu.VMEM((8, 128), jnp.int32),
            pltpu.VMEM((4, 8, 128), jnp.int32),
            pltpu.SMEM((16,), jnp.int32),
            sem((len(STAGES),)),
            sem((K, 2, 5)),
            sem((K, 2, 2)),
            sem((STEPS, 2, 5)),
            sem((STEPS, 2, 5)),
            sem((9,)),
        ],
        compiler_params=pltpu.CompilerParams(
            collective_id=0, has_side_effects=True, vmem_limit_bytes=54 * 1024 * 1024
        ),
    )(
        tokens,
        gate_up.reshape(128, 16, 2 * HID),
        down.reshape(128, 16, HID),
        routes.transpose(0, 2, 1),
        gates.transpose(0, 2, 1),
        expert_load,
        swap_pairs.T,
    )
    return mixed, gu.reshape(1, WIDE, 2 * HID), dn.reshape(1, WIDE, HID), share


def solution(mesh):
    placed = (
        P(None, ("dp", "expert"), None),
        P(None, ("dp", "expert"), None),
        P(None, ("dp", "expert"), None),
        P("expert", None, None),
        P("expert", None, None),
        P("dp", None),
        P(),
    )
    return jax.shard_map(
        on_device,
        mesh=mesh,
        in_specs=placed,
        out_specs=(
            P(None, ("dp", "expert"), None),
            P("expert", None, None),
            P("expert", None, None),
            P("expert"),
        ),
        check_vma=False,
    )
```

```python
import math

import jax
import jax.numpy as jnp
from jax import lax
from jax.experimental import pallas as pl
from jax.experimental.pallas import tpu as pltpu
from jax.sharding import PartitionSpec as P

MESH = pl.DeviceIdType.MESH
STEPS, ROWS, WIDE, HID, TOPK = 4, 16, 2048, 768, 8
HALF = WIDE // 2
QUART = HALF // 2
CW = 384
CHUNKS = [(0, at) for at in range(0, 2 * HID, CW)] + [(1, at) for at in range(0, HID, CW)]
K = len(CHUNKS)
HB = 2

(
    W1, W2, W3, W4, W5, Y1, Y2, Y3, A1, A2, A3, A4, A5, C1, C2, R2, R3, R4, R5, R6, SR, WA, WB, WC, WD,
) = range(25)
X, Z = 0, 1
PLAN = [
    (W1, 3, Z), (A1, 0, X), (W1, 4, X), (W1, 2, X), (A1, 0, Z), (SR, 0, X), (W1, 4, Z), (A2, 0, X), (W1, 2, Z),
    (W2, 3, Z), (W1, 0, X), (A2, 0, Z), (W2, 4, X), (W2, 2, X), (A3, 0, X), (A1, 1, X), (A3, 0, Z), (W3, 3, Z),
    (WA, 0, X), (W3, 4, X), (W4, 3, Z), (W2, 2, Z), (W2, 0, X), (W3, 2, X), (W1, 3, X), (A4, 0, Z), (W4, 4, X),
    (W5, 3, Z), (A2, 1, X), (WB, 0, X), (A1, 1, Z), (A1, 3, X), (W4, 2, X), (W5, 4, X), (W2, 4, Z), (A1, 2, X),
    (W3, 0, X), (A4, 0, X), (A1, 2, Z), (Y1, 3, Z), (W3, 2, Z), (A5, 0, Z), (A2, 1, Z), (W4, 0, X), (W2, 3, X),
    (A3, 1, X), (W5, 2, X), (WC, 0, X), (A2, 3, X), (Y1, 4, X), (A3, 1, Z), (A5, 0, X), (W4, 2, Z), (A1, 3, Z),
    (W1, 0, Z), (W3, 4, Z), (W1, 1, Z), (A2, 2, X), (Y2, 3, Z), (WD, 0, X), (A2, 2, Z), (Y1, 2, X), (W5, 0, X),
    (C1, 0, X), (A4, 1, Z), (W4, 4, Z), (Y2, 4, X), (A4, 1, X), (W5, 2, Z), (C2, 0, X), (W3, 3, X), (W2, 0, Z),
    (A3, 2, X), (Y1, 0, X), (Y2, 2, X), (A5, 1, Z), (A3, 2, Z), (A5, 1, X), (W1, 1, X), (C2, 0, Z), (W2, 1, Z),
    (W5, 4, Z), (W1, 5, X), (W4, 3, X), (Y1, 2, Z), (W1, 5, Z), (A2, 3, Z), (W3, 0, Z), (C1, 1, X), (A4, 2, X),
    (Y1, 4, Z), (W2, 1, X), (A4, 2, Z), (W4, 0, Z), (A3, 3, X), (C2, 1, X), (W5, 3, X), (R2, 0, Z), (Y2, 0, X),
    (W2, 5, Z), (Y2, 2, Z), (W3, 1, Z), (A3, 3, Z), (A5, 2, Z), (A5, 2, X), (C2, 1, Z), (W4, 1, Z), (R2, 0, X),
    (W5, 0, Z), (R2, 1, X), (Y2, 4, Z), (W2, 5, X), (W3, 1, X), (A4, 3, X), (Y1, 3, X), (C1, 2, X), (W4, 1, X),
    (W3, 5, Z), (Y1, 0, Z), (C2, 2, X), (R2, 1, Z), (A4, 3, Z), (W5, 1, Z), (W3, 5, X), (W4, 5, Z), (Y2, 3, X),
    (A5, 3, X), (C2, 2, Z), (R2, 2, X), (R3, 0, Z), (A5, 3, Z), (W5, 1, X), (R3, 1, X), (Y2, 0, Z), (W4, 5, X),
    (R2, 2, Z), (Y1, 1, Z), (R3, 0, X), (W5, 5, Z), (C1, 3, X), (Y1, 1, X), (C2, 3, X), (W5, 5, X), (C2, 3, Z),
    (Y2, 1, Z), (R3, 2, Z), (R2, 3, X), (Y1, 5, Z), (R3, 2, X), (R2, 3, Z), (R4, 0, Z), (R3, 1, Z), (Y3, 4, X),
    (Y3, 2, X), (R3, 3, X), (Y1, 5, X), (R4, 2, Z), (Y2, 1, X), (R3, 3, Z), (Y3, 1, Z), (Y3, 3, X), (R4, 2, X),
    (R4, 1, X), (R4, 1, Z), (Y2, 5, Z), (R4, 0, X), (R5, 2, Z), (R4, 3, X), (R5, 0, Z), (R4, 3, Z), (R5, 2, X),
    (Y3, 2, Z), (R5, 1, Z), (R5, 0, X), (R5, 1, X), (Y2, 5, X), (R5, 3, X), (Y3, 4, Z), (R6, 0, Z), (R5, 3, Z),
    (Y3, 0, Z), (Y3, 1, X), (R6, 2, X), (R6, 2, Z), (R6, 1, Z), (Y3, 5, Z), (R6, 0, X), (Y3, 3, Z), (Y3, 0, X),
    (R6, 1, X), (R6, 3, X), (R6, 3, Z), (Y3, 5, X),
]

STAGES = [
    "W1", "W2", "W3", "W4", "W5", "Y1+", "Y1-", "Y2+", "Y2-",
    "A1+", "A1-", "A2+", "A2-", "A3+", "A3-", "A4+", "A4-", "A5",
    "R1", "R2+", "R2-", "R3+", "R3-", "R4+", "R4-", "R5+", "R5-",
    "WA", "WB", "WC", "L1", "L2", "L3",
]
AT = {name: i for i, name in enumerate(STAGES)}


def kernel(
    tok, gu, dn, routes_in, gates_in, load_in, pairs, mixed, out_gu, out_dn, share, *rest,
):
    full = [rest[2 * k : 2 * k + 2] for k in range(K)]
    (
        buf1, stage, buf3, xs, wgu, wdn, hid, part, sib, t0, t1, zz, u1, t2, v2, t3,
        routes, gates, load, wflat, wsend, wb1, wb2, wb3, wcol, lsend, lrecv, srcs, ss, rw, ry, ra, rr, misc,
    ) = rest[2 * K :]
    y = lax.axis_index("dp")
    e = lax.axis_index("expert")
    x, z, c = e // 8, (e // 2) % 4, e % 2

    def dev(dx=0, dz=0, dc=0, dy=0):
        return (
            lax.rem(y + dy, 4),
            (lax.rem(x + dx, 4) * 4 + lax.rem(z + dz, 4)) * 2 + lax.rem(c + dc, 2),
        )

    def first(h, o):
        return dev(dx=o) if h == 0 else dev(dz=o)

    def second(h, o):
        return dev(dz=o) if h == 0 else dev(dx=o)

    cf = (x, z)
    cg = (z, x)
    sent = {}

    def remote(name, src, dst, rsem, device):
        sent[name] = sent.get(name, 0) + math.prod(src.shape) * 2
        pltpu.make_async_remote_copy(
            src_ref=src, dst_ref=dst, send_sem=ss.at[AT[name]], recv_sem=rsem,
            device_id=device, device_id_type=MESH,
        ).start()

    def local(src, dst, sem):
        pltpu.make_async_copy(src, dst, sem).start()

    def arrived(ref, sem):
        pltpu.make_async_copy(ref, ref, sem).wait()

    def shift(base, o):
        return lax.rem(base + o, 4)

    weights = (gu, dn)
    moved = (out_gu, out_dn)

    def cols(k):
        return pl.ds(CHUNKS[k][1], CW)

    def region(k, h, yy):
        return moved[CHUNKS[k][0]].at[pl.ds(yy * 32 + h * 16, 16), :, cols(k)]

    def W1(k, h):
        for o in (1, 3, 2, 0):
            i = shift(cf[h], o)
            src = weights[CHUNKS[k][0]].at[pl.ds(y * 32 + h * 16 + 4 * i, 4), :, cols(k)]
            dst = buf1.at[k, h, cf[h]]
            if o:
                remote("W1", src, dst, rw.at[k, h, 0], first(h, o))
            else:
                local(src, dst, rw.at[k, h, 0])

    def W2(k, h):
        arrived(buf1.at[k, h], rw.at[k, h, 0])
        for o in (1, 3, 2, 0):
            src = buf1.at[k, h, :, shift(cg[h], o)]
            dst = full[k][h].at[pl.ds(c * 16 + cg[h] * 4, 4)]
            if o:
                remote("W2", src, dst, rw.at[k, h, 1], second(h, o))
            else:
                local(src, dst, rw.at[k, h, 1])

    def W3(k, h):
        mine = full[k][h].at[pl.ds(c * 16, 16)]
        arrived(mine, rw.at[k, h, 1])
        remote("W3", mine, mine, rw.at[k, h, 2], dev(dc=1))

    def W4(k, h):
        arrived(full[k][h].at[pl.ds((1 - c) * 16, 16)], rw.at[k, h, 2])
        for d in range(16):
            s = srcs[d]
            sx, sz, sc = s // 8, (s // 2) % 4, s % 2
            dx, dz = d // 4, d % 4
            if h == 0:
                stage[k, h, dz, dx] = full[k][h][sc * 16 + sz * 4 + sx]
            else:
                stage[k, h, dx, dz] = full[k][h][sc * 16 + sx * 4 + sz]
        for o in (1, 3, 2, 0):
            src = stage.at[k, h, shift(cg[h], o)]
            dst = buf3.at[k, h, cg[h]]
            if o:
                remote("W4", src, dst, rw.at[k, h, 3], second(h, o))
            else:
                local(src, dst, rw.at[k, h, 3])

    def W5(k, h):
        arrived(buf3.at[k, h], rw.at[k, h, 3])
        for o in (1, 3, 2, 0):
            src = buf3.at[k, h, :, shift(cf[h], o)]
            dst = moved[CHUNKS[k][0]].at[pl.ds(y * 32 + h * 16 + 4 * cf[h], 4), :, cols(k)]
            if o:
                remote("W5", src, dst, rw.at[k, h, 4], first(h, o))
            else:
                local(src, dst, rw.at[k, h, 4])

    def Y1(k, h):
        mine = region(k, h, y)
        arrived(mine, rw.at[k, h, 4])
        remote("Y1+", mine, mine, ry.at[k, h, 0], dev(dy=1))
        remote("Y1-", mine, mine, ry.at[k, h, 0], dev(dy=3))

    def Y2(k, h):
        arrived(buf1.at[pl.ds(0, 2), 0], ry.at[k, h, 0])
        up = region(k, h, shift(y, 3)).at[pl.ds(0, 8)]
        remote("Y2+", up, up, ry.at[k, h, 1], dev(dy=1))
        down = region(k, h, shift(y, 1)).at[pl.ds(8, 8)]
        remote("Y2-", down, down, ry.at[k, h, 1], dev(dy=3))

    def Y3(k, h):
        arrived(region(k, h, shift(y, 2)), ry.at[k, h, 1])

    def SR(_, __):
        def one(d, carry):
            slot = d * 2 + c
            total = jnp.int32(0)
            for i in range(16):
                a, b = pairs[0, i], pairs[1, i]
                total = total + jnp.where(a == slot, b, 0) + jnp.where(b == slot, a, 0)
            srcs[d] = total
            return carry

        lax.fori_loop(0, 16, one, 0)

    def side():
        arrived(routes, misc.at[6])
        arrived(gates, misc.at[7])
        arrived(load, misc.at[8])
        expert = lax.broadcasted_iota(jnp.int32, (32, ROWS), 0)
        for s in range(STEPS):
            g = gates[s]
            w = g / jnp.sum(g, axis=0, keepdims=True)
            r = routes[s]
            dense = jnp.zeros((32, ROWS), jnp.float32)
            for t in range(TOPK):
                dense = dense + jnp.where(r[t : t + 1] == expert, w[t : t + 1], 0.0)
            wflat[0:32, s * ROWS : (s + 1) * ROWS] = dense
        for d in range(32):
            wsend[d // 8, (d // 2) % 4, d % 2] = wflat[d : d + 1]
        lsend[...] = jnp.zeros((8, 128), jnp.int32)
        lsend[0:2, 0:32] = load[...]

    def WA(_, __):
        side()
        for o in (1, 3, 2):
            remote("WA", wsend.at[shift(x, o)], wb1.at[x], misc.at[0], dev(dx=o))
        local(wsend.at[x], wb1.at[x], misc.at[0])
        for o in (1, 2, 3):
            remote("L%d" % o, lsend, lrecv.at[y], misc.at[3], dev(dy=o))
        local(lsend, lrecv.at[y], misc.at[3])

    def WB(_, __):
        arrived(wb1, misc.at[0])
        for o in (1, 3, 2):
            remote("WB", wb1.at[:, shift(z, o)], wb2.at[:, z], misc.at[1], dev(dz=o))
        local(wb1.at[:, z], wb2.at[:, z], misc.at[1])

    def WC(_, __):
        arrived(wb2, misc.at[1])
        remote("WC", wb2.at[:, :, 1 - c], wb3.at[c], misc.at[2], dev(dc=1))
        local(wb2.at[:, :, c], wb3.at[c], misc.at[2])

    def WD(_, __):
        arrived(wb3, misc.at[2])
        wflat[...] = jnp.zeros((128, 128), jnp.float32)
        for d in range(32):
            wflat[d : d + 1] = wb3[d // 16, (d // 4) % 4, d % 4]
        wcol[...] = jnp.transpose(wflat[...])
        arrived(lrecv, misc.at[3])
        counts = jnp.sum(jnp.sum(lrecv[...], axis=0), axis=0, keepdims=True)
        lane = lax.broadcasted_iota(jnp.int32, (1, 128), 1)
        mine = jnp.int32(0)
        for i in range(16):
            a, b = pairs[0, i], pairs[1, i]
            mine = mine + jnp.where(a == e, b, 0) + jnp.where(b == e, a, 0)
        asf = counts.astype(jnp.float32)
        own = jnp.sum(jnp.where(lane == mine, asf, 0.0))
        share[0] = own / (jnp.sum(asf) / 32.0)

    def at_f(s, h, i):
        return xs.at[s, h, c, i, z] if h == 0 else xs.at[s, h, c, x, i]

    def line(s, h, i):
        return xs.at[s, h, c, :, i] if h == 0 else xs.at[s, h, c, i]

    LO, HI = pl.ds(0, QUART), pl.ds(QUART, QUART)

    def A1(s, h):
        src = tok.at[s, :, pl.ds(h * HALF, HALF)]
        dst = xs.at[s, h, c, x, z]
        remote("A1+", src, dst, ra.at[s, h, 0], first(h, 1))
        remote("A1-", src, dst, ra.at[s, h, 0], first(h, 3))
        local(src, dst, ra.at[s, h, 0])

    def A2(s, h):
        arrived(xs.at[s, h, 0, 0, pl.ds(0, 3)], ra.at[s, h, 0])
        lo = at_f(s, h, shift(cf[h], 3)).at[:, LO]
        remote("A2+", lo, lo, ra.at[s, h, 1], first(h, 1))
        hi = at_f(s, h, shift(cf[h], 1)).at[:, HI]
        remote("A2-", hi, hi, ra.at[s, h, 1], first(h, 3))

    def A3(s, h):
        arrived(at_f(s, h, shift(cf[h], 2)), ra.at[s, h, 1])
        mine = line(s, h, cg[h])
        remote("A3+", mine, mine, ra.at[s, h, 2], second(h, 1))
        remote("A3-", mine, mine, ra.at[s, h, 2], second(h, 3))

    def A4(s, h):
        arrived(xs.at[s, h, 0, pl.ds(0, 2)], ra.at[s, h, 2])
        lo = line(s, h, shift(cg[h], 3)).at[:, :, LO]
        remote("A4+", lo, lo, ra.at[s, h, 3], second(h, 1))
        hi = line(s, h, shift(cg[h], 1)).at[:, :, HI]
        remote("A4-", hi, hi, ra.at[s, h, 3], second(h, 3))

    def A5(s, h):
        arrived(line(s, h, shift(cg[h], 2)), ra.at[s, h, 3])
        mine = xs.at[s, h, c]
        remote("A5", mine, mine, ra.at[s, h, 4], dev(dc=1))

    loaded = []

    def C1(s, _):
        if not loaded:
            loaded.append(1)
            arrived(wgu, misc.at[4])
            arrived(wdn, misc.at[5])
        for h in (0, 1):
            arrived(xs.at[s, h, 1 - c], ra.at[s, h, 4])

        def tile(n, carry):
            at = pl.multiple_of(n * 256, 256)
            g = jnp.zeros((512, 256), jnp.float32)
            u = jnp.zeros((512, 256), jnp.float32)
            for h in (0, 1):
                rows = xs[s, h].reshape(512, HALF)
                g = g + jnp.dot(
                    rows,
                    wgu[h * 64 : (h + 1) * 64, :, pl.ds(at, 256)].reshape(HALF, 256),
                    preferred_element_type=jnp.float32,
                )
                u = u + jnp.dot(
                    rows,
                    wgu[h * 64 : (h + 1) * 64, :, pl.ds(pl.multiple_of(at + HID, 256), 256)].reshape(HALF, 256),
                    preferred_element_type=jnp.float32,
                )
            hid[s % HB, :, pl.ds(at, 256)] = (g / (1.0 + jnp.exp(-g)) * u).astype(jnp.bfloat16)
            return carry

        lax.fori_loop(0, 3, tile, 0)

    def C2(s, h):
        def tile(j, carry):
            at = pl.multiple_of(j * QUART, QUART)
            o = lax.dot_general(
                hid[s % HB],
                wdn[pl.ds(h * 64 + j * 32, 32)].reshape(QUART, HID),
                (((1,), (1,)), ((), ())),
                preferred_element_type=jnp.float32,
            )
            for d in range(32):
                w = wcol[s * ROWS : (s + 1) * ROWS, d : d + 1]
                piece = (o[d * ROWS : (d + 1) * ROWS] * w).astype(jnp.bfloat16)
                part[s, h, d // 16, (d // 4) % 4, d % 4, :, pl.ds(at, QUART)] = piece
            return carry

        lax.fori_loop(0, 2, tile, 0)
        remote("R1", part.at[s, h, 1 - c], sib.at[s, h], rr.at[s, h, 0], dev(dc=1))

    def f32(v):
        return v.astype(jnp.float32)

    def b16(v):
        return v.astype(jnp.bfloat16)

    def chip(s, h, i):
        if h == 0:
            return f32(part[s, h, c, i]) + f32(sib[s, h, i])
        return f32(part[s, h, c, :, i]) + f32(sib[s, h, :, i])

    def mine(s, h, i):
        return part.at[s, h, c, i] if h == 0 else part.at[s, h, c, :, i]

    def keep(s, h, i, cut, value):
        if h == 0:
            part[s, h, c, i, :, :, cut] = b16(value)
        else:
            part[s, h, c, :, i, :, cut] = b16(value)

    def R2(s, h):
        arrived(sib.at[s, h], rr.at[s, h, 0])
        i = shift(cf[h], 2)
        keep(s, h, i, slice(0, HALF), chip(s, h, i))
        remote("R2+", mine(s, h, i).at[:, :, LO], t0.at[s, h, :, :, LO], rr.at[s, h, 1], first(h, 1))
        remote("R2-", mine(s, h, i).at[:, :, HI], t0.at[s, h, :, :, HI], rr.at[s, h, 1], first(h, 3))

    def R3(s, h):
        arrived(t0.at[s, h], rr.at[s, h, 1])
        i = shift(cf[h], 1)
        v = chip(s, h, i)
        keep(s, h, i, slice(0, QUART), v[:, :, 0:QUART] + f32(t0[s, h, :, :, 0:QUART]))
        keep(s, h, i, slice(QUART, HALF), v[:, :, QUART:HALF])
        remote("R3+", mine(s, h, i), t1.at[s, h, 0], rr.at[s, h, 2], first(h, 1))
        i = shift(cf[h], 3)
        v = chip(s, h, i)
        keep(s, h, i, slice(0, QUART), v[:, :, 0:QUART])
        keep(s, h, i, slice(QUART, HALF), v[:, :, QUART:HALF] + f32(t0[s, h, :, :, QUART:HALF]))
        remote("R3-", mine(s, h, i), t1.at[s, h, 1], rr.at[s, h, 2], first(h, 3))

    def R4(s, h):
        arrived(t1.at[s, h], rr.at[s, h, 2])
        zz[s, h] = chip(s, h, cf[h]) + f32(t1[s, h, 0]) + f32(t1[s, h, 1])
        u1[s, h] = b16(zz[s, h, shift(cg[h], 2)])
        remote("R4+", u1.at[s, h, :, LO], t2.at[s, h, :, LO], rr.at[s, h, 3], second(h, 1))
        remote("R4-", u1.at[s, h, :, HI], t2.at[s, h, :, HI], rr.at[s, h, 3], second(h, 3))

    def R5(s, h):
        arrived(t2.at[s, h], rr.at[s, h, 3])
        v = zz[s, h, shift(cg[h], 1)]
        v2[s, h, 0, :, 0:QUART] = b16(v[:, 0:QUART] + f32(t2[s, h, :, 0:QUART]))
        v2[s, h, 0, :, QUART:HALF] = b16(v[:, QUART:HALF])
        remote("R5+", v2.at[s, h, 0], t3.at[s, h, 0], rr.at[s, h, 4], second(h, 1))
        v = zz[s, h, shift(cg[h], 3)]
        v2[s, h, 1, :, 0:QUART] = b16(v[:, 0:QUART])
        v2[s, h, 1, :, QUART:HALF] = b16(v[:, QUART:HALF] + f32(t2[s, h, :, QUART:HALF]))
        remote("R5-", v2.at[s, h, 1], t3.at[s, h, 1], rr.at[s, h, 4], second(h, 3))

    def R6(s, h):
        arrived(t3.at[s, h], rr.at[s, h, 4])
        mixed[s, :, h * HALF : (h + 1) * HALF] = zz[s, h, cg[h]] + f32(t3[s, h, 0]) + f32(t3[s, h, 1])

    bar = pltpu.get_barrier_semaphore()
    peers = [dev(dc=1)]
    for o in (1, 2, 3):
        peers += [dev(dx=o), dev(dz=o), dev(dy=o)]
    for peer in peers:
        pl.semaphore_signal(bar, inc=1, device_id=peer, device_id_type=MESH)
    for n, (src, dst) in enumerate(((routes_in, routes), (gates_in, gates), (load_in, load))):
        local(src, dst, misc.at[6 + n])
    pl.semaphore_wait(bar, len(peers))

    tasks = (
        W1, W2, W3, W4, W5, Y1, Y2, Y3, A1, A2, A3, A4, A5, C1, C2, R2, R3, R4, R5, R6, SR, WA, WB, WC, WD,
    )
    for number, item in enumerate(PLAN):
        stage_of, index, half = item
        tasks[stage_of](index, half)
        if number == 8:
            local(gu, wgu, misc.at[4])
            local(dn, wdn, misc.at[5])

    total = dict(
        {name: buf1.at[:, :, pl.ds(0, 3)] for name in ("W1", "W2", "W4", "W5")},
        **{name: buf1 for name in ("W3", "Y1+", "Y1-")},
        **{name: buf1.at[:, 0] for name in ("Y2+", "Y2-")},
        **{name: u1 for name in ("A1+", "A1-")},
        **{name: u1.at[:, :, :, LO] for name in ("A2+", "A2-", "R4+", "R4-")},
        **{name: t0 for name in ("A3+", "A3-", "R3+", "R3-")},
        **{name: t0.at[:, :, :, :, LO] for name in ("A4+", "A4-", "R2+", "R2-")},
        **{name: sib for name in ("A5", "R1")},
        **{name: u1 for name in ("R5+", "R5-")},
        WA=wsend.at[pl.ds(0, 3)], WB=wb1.at[:, pl.ds(0, 3)], WC=wb3.at[0],
        L1=lsend, L2=lsend, L3=lsend,
    )
    for name in sent:
        assert math.prod(total[name].shape) * 2 == sent[name], name
        arrived(total[name], ss.at[AT[name]])


def copy_out(m_in, g_in, d_in, s_in, m_out, g_out, d_out, s_out, sems):
    pairs = [(m_in, m_out)]
    for i in range(4):
        cut = pl.ds(32 * i, 32)
        pairs += [(g_in.at[cut], g_out.at[cut]), (d_in.at[cut], d_out.at[cut])]
    copies = [pltpu.make_async_copy(a, b, sems.at[n]) for n, (a, b) in enumerate(pairs)]
    for copy in copies:
        copy.start()
    s_out[0] = s_in[0]
    for copy in copies:
        copy.wait()


def on_device(tokens, routes, gates, gate_up, down, expert_load, swap_pairs):
    hbm = pl.BlockSpec(memory_space=pltpu.HBM)
    vmem = pl.BlockSpec(memory_space=pltpu.VMEM)
    smem = pl.BlockSpec(memory_space=pltpu.SMEM)
    bf, f = jnp.bfloat16, jnp.float32
    sem = pltpu.SemaphoreType.DMA
    shapes = (
        jax.ShapeDtypeStruct((STEPS, ROWS, WIDE), f),
        jax.ShapeDtypeStruct((128, 16, 2 * HID), bf),
        jax.ShapeDtypeStruct((128, 16, HID), bf),
        jax.ShapeDtypeStruct((1,), f),
    )
    mixed, gu, dn, share = pl.pallas_call(
        kernel,
        out_shape=(pltpu.VMEM(shapes[0].shape, f), pltpu.VMEM(shapes[1].shape, bf), pltpu.VMEM(shapes[2].shape, bf), shapes[3]),
        in_specs=[hbm, hbm, hbm, hbm, hbm, hbm, smem],
        out_specs=(vmem, vmem, vmem, smem),
        scratch_shapes=[
            *[pltpu.VMEM((32, 16, CW), bf)] * (2 * K),
            pltpu.VMEM((K, 2, 4, 4, 16, CW), bf),
            pltpu.VMEM((K, 2, 4, 4, 16, CW), bf),
            pltpu.VMEM((K, 2, 4, 4, 16, CW), bf),
            pltpu.VMEM((STEPS, 2, 2, 4, 4, ROWS, HALF), bf),
            pltpu.VMEM((128, 16, 2 * HID), bf),
            pltpu.VMEM((128, 16, HID), bf),
            pltpu.VMEM((HB, 512, HID), bf),
            pltpu.VMEM((STEPS, 2, 2, 4, 4, ROWS, HALF), bf),
            pltpu.VMEM((STEPS, 2, 4, 4, ROWS, HALF), bf),
            pltpu.VMEM((STEPS, 2, 4, ROWS, HALF), bf),
            pltpu.VMEM((STEPS, 2, 2, 4, ROWS, HALF), bf),
            pltpu.VMEM((STEPS, 2, 4, ROWS, HALF), f),
            pltpu.VMEM((STEPS, 2, ROWS, HALF), bf),
            pltpu.VMEM((STEPS, 2, ROWS, HALF), bf),
            pltpu.VMEM((STEPS, 2, 2, ROWS, HALF), bf),
            pltpu.VMEM((STEPS, 2, 2, ROWS, HALF), bf),
            pltpu.VMEM((STEPS, TOPK, ROWS), jnp.int32),
            pltpu.VMEM((STEPS, TOPK, ROWS), f),
            pltpu.VMEM((2, 32), jnp.int32),
            pltpu.VMEM((128, 128), f),
            pltpu.VMEM((4, 4, 2, 1, 128), f),
            pltpu.VMEM((4, 4, 2, 1, 128), f),
            pltpu.VMEM((4, 4, 2, 1, 128), f),
            pltpu.VMEM((2, 4, 4, 1, 128), f),
            pltpu.VMEM((128, 128), f),
            pltpu.VMEM((8, 128), jnp.int32),
            pltpu.VMEM((4, 8, 128), jnp.int32),
            pltpu.SMEM((16,), jnp.int32),
            sem((len(STAGES),)),
            sem((K, 2, 5)),
            sem((K, 2, 2)),
            sem((STEPS, 2, 5)),
            sem((STEPS, 2, 5)),
            sem((9,)),
        ],
        compiler_params=pltpu.CompilerParams(
            collective_id=0, has_side_effects=True, vmem_limit_bytes=54 * 1024 * 1024
        ),
    )(
        tokens,
        gate_up.reshape(128, 16, 2 * HID),
        down.reshape(128, 16, HID),
        routes.transpose(0, 2, 1),
        gates.transpose(0, 2, 1),
        expert_load,
        swap_pairs.T,
    )
    mixed, gu, dn = (pltpu.with_memory_space_constraint(v, pltpu.VMEM) for v in (mixed, gu, dn))
    mixed, gu, dn, share = pl.pallas_call(
        copy_out,
        out_shape=shapes,
        in_specs=[vmem, vmem, vmem, smem],
        out_specs=(hbm, hbm, hbm, smem),
        scratch_shapes=[sem((9,))],
        compiler_params=pltpu.CompilerParams(vmem_limit_bytes=4 * 1024 * 1024),
    )(mixed, gu, dn, share)
    return mixed, gu.reshape(1, WIDE, 2 * HID), dn.reshape(1, WIDE, HID), share


def solution(mesh):
    placed = (
        P(None, ("dp", "expert"), None),
        P(None, ("dp", "expert"), None),
        P(None, ("dp", "expert"), None),
        P("expert", None, None),
        P("expert", None, None),
        P("dp", None),
        P(),
    )
    return jax.shard_map(
        on_device,
        mesh=mesh,
        in_specs=placed,
        out_specs=(
            P(None, ("dp", "expert"), None),
            P("expert", None, None),
            P("expert", None, None),
            P("expert"),
        ),
        check_vma=False,
    )
```

```python
import math

import jax
import jax.numpy as jnp
from jax import lax
from jax.experimental import pallas as pl
from jax.experimental.pallas import tpu as pltpu
from jax.sharding import PartitionSpec as P

MESH = pl.DeviceIdType.MESH
STEPS, ROWS, WIDE, HID, TOPK = 4, 16, 2048, 768, 8
HALF = WIDE // 2
QUART = HALF // 2
CW = 384
CHUNKS = [(0, at) for at in range(0, 2 * HID, CW)] + [(1, at) for at in range(0, HID, CW)]
K = len(CHUNKS)
HB = 2

(
    W1, W2, W3, W4, W5, Y1, Y2, Y3, A1, A2, A3, A4, A5, C1, C2, R2, R3, R4, R5, R6, SR, WA, WB, WC, WD,
) = range(25)
X, Z = 0, 1
PLAN = [
    (W1, 3, Z), (A1, 0, X), (W1, 4, X), (W1, 2, X), (A1, 0, Z), (SR, 0, X), (W1, 4, Z), (A2, 0, X), (W1, 2, Z),
    (W2, 3, Z), (W1, 0, X), (A2, 0, Z), (W2, 4, X), (W2, 2, X), (A3, 0, X), (A1, 1, X), (A3, 0, Z), (W3, 3, Z),
    (WA, 0, X), (W3, 4, X), (W4, 3, Z), (W2, 2, Z), (W2, 0, X), (W3, 2, X), (W1, 3, X), (A4, 0, Z), (W4, 4, X),
    (W5, 3, Z), (A2, 1, X), (WB, 0, X), (A1, 1, Z), (A1, 3, X), (W4, 2, X), (W5, 4, X), (W2, 4, Z), (A1, 2, X),
    (W3, 0, X), (A4, 0, X), (A1, 2, Z), (Y1, 3, Z), (W3, 2, Z), (A5, 0, Z), (A2, 1, Z), (W4, 0, X), (W2, 3, X),
    (A3, 1, X), (W5, 2, X), (WC, 0, X), (A2, 3, X), (Y1, 4, X), (A3, 1, Z), (A5, 0, X), (W4, 2, Z), (A1, 3, Z),
    (W1, 0, Z), (W3, 4, Z), (W1, 1, Z), (A2, 2, X), (Y2, 3, Z), (WD, 0, X), (A2, 2, Z), (Y1, 2, X), (W5, 0, X),
    (C1, 0, X), (A4, 1, Z), (W4, 4, Z), (Y2, 4, X), (A4, 1, X), (W5, 2, Z), (C2, 0, X), (W3, 3, X), (W2, 0, Z),
    (A3, 2, X), (Y1, 0, X), (Y2, 2, X), (A5, 1, Z), (A3, 2, Z), (A5, 1, X), (W1, 1, X), (C2, 0, Z), (W2, 1, Z),
    (W5, 4, Z), (W1, 5, X), (W4, 3, X), (Y1, 2, Z), (W1, 5, Z), (A2, 3, Z), (W3, 0, Z), (C1, 1, X), (A4, 2, X),
    (Y1, 4, Z), (W2, 1, X), (A4, 2, Z), (W4, 0, Z), (A3, 3, X), (C2, 1, X), (W5, 3, X), (R2, 0, Z), (Y2, 0, X),
    (W2, 5, Z), (Y2, 2, Z), (W3, 1, Z), (A3, 3, Z), (A5, 2, Z), (A5, 2, X), (C2, 1, Z), (W4, 1, Z), (R2, 0, X),
    (W5, 0, Z), (R2, 1, X), (Y2, 4, Z), (W2, 5, X), (W3, 1, X), (A4, 3, X), (Y1, 3, X), (C1, 2, X), (W4, 1, X),
    (W3, 5, Z), (Y1, 0, Z), (C2, 2, X), (R2, 1, Z), (A4, 3, Z), (W5, 1, Z), (W3, 5, X), (W4, 5, Z), (Y2, 3, X),
    (A5, 3, X), (C2, 2, Z), (R2, 2, X), (R3, 0, Z), (A5, 3, Z), (W5, 1, X), (R3, 1, X), (Y2, 0, Z), (W4, 5, X),
    (R2, 2, Z), (Y1, 1, Z), (R3, 0, X), (W5, 5, Z), (C1, 3, X), (Y1, 1, X), (C2, 3, X), (W5, 5, X), (C2, 3, Z),
    (Y2, 1, Z), (R3, 2, Z), (R2, 3, X), (Y1, 5, Z), (R3, 2, X), (R2, 3, Z), (R4, 0, Z), (R3, 1, Z), (Y3, 4, X),
    (Y3, 2, X), (R3, 3, X), (Y1, 5, X), (R4, 2, Z), (Y2, 1, X), (R3, 3, Z), (Y3, 1, Z), (Y3, 3, X), (R4, 2, X),
    (R4, 1, X), (R4, 1, Z), (Y2, 5, Z), (R4, 0, X), (R5, 2, Z), (R4, 3, X), (R5, 0, Z), (R4, 3, Z), (R5, 2, X),
    (Y3, 2, Z), (R5, 1, Z), (R5, 0, X), (R5, 1, X), (Y2, 5, X), (R5, 3, X), (Y3, 4, Z), (R6, 0, Z), (R5, 3, Z),
    (Y3, 0, Z), (Y3, 1, X), (R6, 2, X), (R6, 2, Z), (R6, 1, Z), (Y3, 5, Z), (R6, 0, X), (Y3, 3, Z), (Y3, 0, X),
    (R6, 1, X), (R6, 3, X), (R6, 3, Z), (Y3, 5, X),
]

STAGES = [
    "W1", "W2", "W3", "W4", "W5", "Y1+", "Y1-", "Y2+", "Y2-",
    "A1+", "A1-", "A2+", "A2-", "A3+", "A3-", "A4+", "A4-", "A5",
    "R1", "R2+", "R2-", "R3+", "R3-", "R4+", "R4-", "R5+", "R5-",
    "WA", "WB", "WC", "L1", "L2", "L3",
]
AT = {name: i for i, name in enumerate(STAGES)}


def kernel(
    tok, gu, dn, routes_in, gates_in, load_in, pairs, mixed, out_gu, out_dn, share, *rest,
):
    full = [rest[2 * k : 2 * k + 2] for k in range(K)]
    (
        buf1, stage, buf3, xs, wgu, wdn, hid, part, sib, t0, t1, zz, u1, t2, v2, t3,
        routes, gates, load, wflat, wsend, wb1, wb2, wb3, wcol, lsend, lrecv, srcs, ss, rw, ry, ra, misc,
    ) = rest[2 * K :]
    y = lax.axis_index("dp")
    e = lax.axis_index("expert")
    x, z, c = e // 8, (e // 2) % 4, e % 2

    def dev(dx=0, dz=0, dc=0, dy=0):
        return (
            lax.rem(y + dy, 4),
            (lax.rem(x + dx, 4) * 4 + lax.rem(z + dz, 4)) * 2 + lax.rem(c + dc, 2),
        )

    def first(h, o):
        return dev(dx=o) if h == 0 else dev(dz=o)

    def second(h, o):
        return dev(dz=o) if h == 0 else dev(dx=o)

    cf = (x, z)
    cg = (z, x)
    sent = {}

    def remote(name, src, dst, rsem, device):
        sent[name] = sent.get(name, 0) + math.prod(src.shape) * 2
        pltpu.make_async_remote_copy(
            src_ref=src, dst_ref=dst, send_sem=ss.at[AT[name]], recv_sem=rsem,
            device_id=device, device_id_type=MESH,
        ).start()

    def local(src, dst, sem):
        pltpu.make_async_copy(src, dst, sem).start()

    def arrived(ref, sem):
        pltpu.make_async_copy(ref, ref, sem).wait()

    def shift(base, o):
        return lax.rem(base + o, 4)

    weights = (gu, dn)
    moved = (out_gu, out_dn)

    def cols(k):
        return pl.ds(CHUNKS[k][1], CW)

    def region(k, h, yy):
        return moved[CHUNKS[k][0]].at[pl.ds(yy * 32 + h * 16, 16), :, cols(k)]

    def W1(k, h):
        for o in (1, 3, 2, 0):
            i = shift(cf[h], o)
            src = weights[CHUNKS[k][0]].at[pl.ds(y * 32 + h * 16 + 4 * i, 4), :, cols(k)]
            dst = buf1.at[k, h, cf[h]]
            if o:
                remote("W1", src, dst, rw.at[k, h, 0], first(h, o))
            else:
                local(src, dst, rw.at[k, h, 0])

    def W2(k, h):
        arrived(buf1.at[k, h], rw.at[k, h, 0])
        for o in (1, 3, 2, 0):
            src = buf1.at[k, h, :, shift(cg[h], o)]
            dst = full[k][h].at[pl.ds(c * 16 + cg[h] * 4, 4)]
            if o:
                remote("W2", src, dst, rw.at[k, h, 1], second(h, o))
            else:
                local(src, dst, rw.at[k, h, 1])

    def W3(k, h):
        mine = full[k][h].at[pl.ds(c * 16, 16)]
        arrived(mine, rw.at[k, h, 1])
        remote("W3", mine, mine, rw.at[k, h, 2], dev(dc=1))

    def W4(k, h):
        arrived(full[k][h].at[pl.ds((1 - c) * 16, 16)], rw.at[k, h, 2])
        for d in range(16):
            s = srcs[d]
            sx, sz, sc = s // 8, (s // 2) % 4, s % 2
            dx, dz = d // 4, d % 4
            if h == 0:
                stage[k, h, dz, dx] = full[k][h][sc * 16 + sz * 4 + sx]
            else:
                stage[k, h, dx, dz] = full[k][h][sc * 16 + sx * 4 + sz]
        for o in (1, 3, 2, 0):
            src = stage.at[k, h, shift(cg[h], o)]
            dst = buf3.at[k, h, cg[h]]
            if o:
                remote("W4", src, dst, rw.at[k, h, 3], second(h, o))
            else:
                local(src, dst, rw.at[k, h, 3])

    def W5(k, h):
        arrived(buf3.at[k, h], rw.at[k, h, 3])
        for o in (1, 3, 2, 0):
            src = buf3.at[k, h, :, shift(cf[h], o)]
            dst = moved[CHUNKS[k][0]].at[pl.ds(y * 32 + h * 16 + 4 * cf[h], 4), :, cols(k)]
            if o:
                remote("W5", src, dst, rw.at[k, h, 4], first(h, o))
            else:
                local(src, dst, rw.at[k, h, 4])

    def Y1(k, h):
        mine = region(k, h, y)
        arrived(mine, rw.at[k, h, 4])
        remote("Y1+", mine, mine, ry.at[k, h, 0], dev(dy=1))
        remote("Y1-", mine, mine, ry.at[k, h, 0], dev(dy=3))

    def Y2(k, h):
        arrived(buf1.at[pl.ds(0, 2), 0], ry.at[k, h, 0])
        up = region(k, h, shift(y, 3)).at[pl.ds(0, 8)]
        remote("Y2+", up, up, ry.at[k, h, 1], dev(dy=1))
        down = region(k, h, shift(y, 1)).at[pl.ds(8, 8)]
        remote("Y2-", down, down, ry.at[k, h, 1], dev(dy=3))

    def Y3(k, h):
        arrived(region(k, h, shift(y, 2)), ry.at[k, h, 1])

    def SR(_, __):
        def one(d, carry):
            slot = d * 2 + c
            total = jnp.int32(0)
            for i in range(16):
                a, b = pairs[0, i], pairs[1, i]
                total = total + jnp.where(a == slot, b, 0) + jnp.where(b == slot, a, 0)
            srcs[d] = total
            return carry

        lax.fori_loop(0, 16, one, 0)

    def side():
        arrived(routes, misc.at[6])
        arrived(gates, misc.at[7])
        arrived(load, misc.at[8])
        expert = lax.broadcasted_iota(jnp.int32, (32, ROWS), 0)
        for s in range(STEPS):
            g = gates[s]
            w = g / jnp.sum(g, axis=0, keepdims=True)
            r = routes[s]
            dense = jnp.zeros((32, ROWS), jnp.float32)
            for t in range(TOPK):
                dense = dense + jnp.where(r[t : t + 1] == expert, w[t : t + 1], 0.0)
            wflat[0:32, s * ROWS : (s + 1) * ROWS] = dense
        for d in range(32):
            wsend[d // 8, (d // 2) % 4, d % 2] = wflat[d : d + 1]
        lsend[...] = jnp.zeros((8, 128), jnp.int32)
        lsend[0:2, 0:32] = load[...]

    def WA(_, __):
        side()
        for o in (1, 3, 2):
            remote("WA", wsend.at[shift(x, o)], wb1.at[x], misc.at[0], dev(dx=o))
        local(wsend.at[x], wb1.at[x], misc.at[0])
        for o in (1, 2, 3):
            remote("L%d" % o, lsend, lrecv.at[y], misc.at[3], dev(dy=o))
        local(lsend, lrecv.at[y], misc.at[3])

    def WB(_, __):
        arrived(wb1, misc.at[0])
        for o in (1, 3, 2):
            remote("WB", wb1.at[:, shift(z, o)], wb2.at[:, z], misc.at[1], dev(dz=o))
        local(wb1.at[:, z], wb2.at[:, z], misc.at[1])

    def WC(_, __):
        arrived(wb2, misc.at[1])
        remote("WC", wb2.at[:, :, 1 - c], wb3.at[c], misc.at[2], dev(dc=1))
        local(wb2.at[:, :, c], wb3.at[c], misc.at[2])

    def WD(_, __):
        arrived(wb3, misc.at[2])
        wflat[...] = jnp.zeros((128, 128), jnp.float32)
        for d in range(32):
            wflat[d : d + 1] = wb3[d // 16, (d // 4) % 4, d % 4]
        wcol[...] = jnp.transpose(wflat[...])
        arrived(lrecv, misc.at[3])
        counts = jnp.sum(jnp.sum(lrecv[...], axis=0), axis=0, keepdims=True)
        lane = lax.broadcasted_iota(jnp.int32, (1, 128), 1)
        mine = jnp.int32(0)
        for i in range(16):
            a, b = pairs[0, i], pairs[1, i]
            mine = mine + jnp.where(a == e, b, 0) + jnp.where(b == e, a, 0)
        asf = counts.astype(jnp.float32)
        own = jnp.sum(jnp.where(lane == mine, asf, 0.0))
        share[0] = own / (jnp.sum(asf) / 32.0)

    def at_f(s, h, i):
        return xs.at[s, h, c, i, z] if h == 0 else xs.at[s, h, c, x, i]

    def line(s, h, i):
        return xs.at[s, h, c, :, i] if h == 0 else xs.at[s, h, c, i]

    LO, HI = pl.ds(0, QUART), pl.ds(QUART, QUART)

    def A1(s, h):
        src = tok.at[s, :, pl.ds(h * HALF, HALF)]
        dst = xs.at[s, h, c, x, z]
        remote("A1+", src, dst, ra.at[s, h, 0], first(h, 1))
        remote("A1-", src, dst, ra.at[s, h, 0], first(h, 3))
        local(src, dst, ra.at[s, h, 0])

    def A2(s, h):
        arrived(xs.at[s, h, 0, 0, pl.ds(0, 3)], ra.at[s, h, 0])
        lo = at_f(s, h, shift(cf[h], 3)).at[:, LO]
        remote("A2+", lo, lo, ra.at[s, h, 1], first(h, 1))
        hi = at_f(s, h, shift(cf[h], 1)).at[:, HI]
        remote("A2-", hi, hi, ra.at[s, h, 1], first(h, 3))

    def A3(s, h):
        arrived(at_f(s, h, shift(cf[h], 2)), ra.at[s, h, 1])
        mine = line(s, h, cg[h])
        remote("A3+", mine, mine, ra.at[s, h, 2], second(h, 1))
        remote("A3-", mine, mine, ra.at[s, h, 2], second(h, 3))

    def A4(s, h):
        arrived(xs.at[s, h, 0, pl.ds(0, 2)], ra.at[s, h, 2])
        lo = line(s, h, shift(cg[h], 3)).at[:, :, LO]
        remote("A4+", lo, lo, ra.at[s, h, 3], second(h, 1))
        hi = line(s, h, shift(cg[h], 1)).at[:, :, HI]
        remote("A4-", hi, hi, ra.at[s, h, 3], second(h, 3))

    def A5(s, h):
        arrived(line(s, h, shift(cg[h], 2)), ra.at[s, h, 3])
        mine = xs.at[s, h, c]
        remote("A5", mine, mine, ra.at[s, h, 4], dev(dc=1))

    loaded = []

    def C1(s, _):
        if not loaded:
            loaded.append(1)
            arrived(wgu, misc.at[4])
            arrived(wdn, misc.at[5])
        for h in (0, 1):
            arrived(xs.at[s, h, 1 - c], ra.at[s, h, 4])

        def tile(n, carry):
            at = pl.multiple_of(n * 256, 256)
            g = jnp.zeros((512, 256), jnp.float32)
            u = jnp.zeros((512, 256), jnp.float32)
            for h in (0, 1):
                rows = xs[s, h].reshape(512, HALF)
                g = g + jnp.dot(
                    rows,
                    wgu[h * 64 : (h + 1) * 64, :, pl.ds(at, 256)].reshape(HALF, 256),
                    preferred_element_type=jnp.float32,
                )
                u = u + jnp.dot(
                    rows,
                    wgu[h * 64 : (h + 1) * 64, :, pl.ds(pl.multiple_of(at + HID, 256), 256)].reshape(HALF, 256),
                    preferred_element_type=jnp.float32,
                )
            hid[s % HB, :, pl.ds(at, 256)] = (g / (1.0 + jnp.exp(-g)) * u).astype(jnp.bfloat16)
            return carry

        lax.fori_loop(0, 3, tile, 0)

    def C2(s, h):
        def tile(j, carry):
            at = pl.multiple_of(j * QUART, QUART)
            o = lax.dot_general(
                hid[s % HB],
                wdn[pl.ds(h * 64 + j * 32, 32)].reshape(QUART, HID),
                (((1,), (1,)), ((), ())),
                preferred_element_type=jnp.float32,
            )
            for d in range(32):
                w = wcol[s * ROWS : (s + 1) * ROWS, d : d + 1]
                piece = (o[d * ROWS : (d + 1) * ROWS] * w).astype(jnp.bfloat16)
                part[s, h, d // 16, (d // 4) % 4, d % 4, :, pl.ds(at, QUART)] = piece
            return carry

        lax.fori_loop(0, 2, tile, 0)
        remote("R1", part.at[s, h, 1 - c], sib.at[s, h], ra.at[s, h, 0], dev(dc=1))

    def f32(v):
        return v.astype(jnp.float32)

    def b16(v):
        return v.astype(jnp.bfloat16)

    def chip(s, h, i):
        if h == 0:
            return f32(part[s, h, c, i]) + f32(sib[s, h, i])
        return f32(part[s, h, c, :, i]) + f32(sib[s, h, :, i])

    def mine(s, h, i):
        return part.at[s, h, c, i] if h == 0 else part.at[s, h, c, :, i]

    def keep(s, h, i, cut, value):
        if h == 0:
            part[s, h, c, i, :, :, cut] = b16(value)
        else:
            part[s, h, c, :, i, :, cut] = b16(value)

    def R2(s, h):
        arrived(sib.at[s, h], ra.at[s, h, 0])
        i = shift(cf[h], 2)
        keep(s, h, i, slice(0, HALF), chip(s, h, i))
        remote("R2+", mine(s, h, i).at[:, :, LO], t0.at[s, h, :, :, LO], ra.at[s, h, 1], first(h, 1))
        remote("R2-", mine(s, h, i).at[:, :, HI], t0.at[s, h, :, :, HI], ra.at[s, h, 1], first(h, 3))

    def R3(s, h):
        arrived(t0.at[s, h], ra.at[s, h, 1])
        i = shift(cf[h], 1)
        v = chip(s, h, i)
        keep(s, h, i, slice(0, QUART), v[:, :, 0:QUART] + f32(t0[s, h, :, :, 0:QUART]))
        keep(s, h, i, slice(QUART, HALF), v[:, :, QUART:HALF])
        remote("R3+", mine(s, h, i), t1.at[s, h, 0], ra.at[s, h, 2], first(h, 1))
        i = shift(cf[h], 3)
        v = chip(s, h, i)
        keep(s, h, i, slice(0, QUART), v[:, :, 0:QUART])
        keep(s, h, i, slice(QUART, HALF), v[:, :, QUART:HALF] + f32(t0[s, h, :, :, QUART:HALF]))
        remote("R3-", mine(s, h, i), t1.at[s, h, 1], ra.at[s, h, 2], first(h, 3))

    def R4(s, h):
        arrived(t1.at[s, h], ra.at[s, h, 2])
        zz[s, h] = chip(s, h, cf[h]) + f32(t1[s, h, 0]) + f32(t1[s, h, 1])
        u1[s, h] = b16(zz[s, h, shift(cg[h], 2)])
        remote("R4+", u1.at[s, h, :, LO], t2.at[s, h, :, LO], ra.at[s, h, 3], second(h, 1))
        remote("R4-", u1.at[s, h, :, HI], t2.at[s, h, :, HI], ra.at[s, h, 3], second(h, 3))

    def R5(s, h):
        arrived(t2.at[s, h], ra.at[s, h, 3])
        v = zz[s, h, shift(cg[h], 1)]
        v2[s, h, 0, :, 0:QUART] = b16(v[:, 0:QUART] + f32(t2[s, h, :, 0:QUART]))
        v2[s, h, 0, :, QUART:HALF] = b16(v[:, QUART:HALF])
        remote("R5+", v2.at[s, h, 0], t3.at[s, h, 0], ra.at[s, h, 4], second(h, 1))
        v = zz[s, h, shift(cg[h], 3)]
        v2[s, h, 1, :, 0:QUART] = b16(v[:, 0:QUART])
        v2[s, h, 1, :, QUART:HALF] = b16(v[:, QUART:HALF] + f32(t2[s, h, :, QUART:HALF]))
        remote("R5-", v2.at[s, h, 1], t3.at[s, h, 1], ra.at[s, h, 4], second(h, 3))

    def R6(s, h):
        arrived(t3.at[s, h], ra.at[s, h, 4])
        mixed[s, :, h * HALF : (h + 1) * HALF] = zz[s, h, cg[h]] + f32(t3[s, h, 0]) + f32(t3[s, h, 1])

    bar = pltpu.get_barrier_semaphore()
    peers = [dev(dc=1)]
    for o in (1, 2, 3):
        peers += [dev(dx=o), dev(dz=o), dev(dy=o)]
    for peer in peers:
        pl.semaphore_signal(bar, inc=1, device_id=peer, device_id_type=MESH)
    for n, (src, dst) in enumerate(((routes_in, routes), (gates_in, gates), (load_in, load))):
        local(src, dst, misc.at[6 + n])
    pl.semaphore_wait(bar, len(peers))

    tasks = (
        W1, W2, W3, W4, W5, Y1, Y2, Y3, A1, A2, A3, A4, A5, C1, C2, R2, R3, R4, R5, R6, SR, WA, WB, WC, WD,
    )
    for number, item in enumerate(PLAN):
        stage_of, index, half = item
        tasks[stage_of](index, half)
        if number == 8:
            local(gu, wgu, misc.at[4])
            local(dn, wdn, misc.at[5])

    total = dict(
        {name: buf1.at[:, :, pl.ds(0, 3)] for name in ("W1", "W2", "W4", "W5")},
        **{name: buf1 for name in ("W3", "Y1+", "Y1-")},
        **{name: buf1.at[:, 0] for name in ("Y2+", "Y2-")},
        **{name: u1 for name in ("A1+", "A1-")},
        **{name: u1.at[:, :, :, LO] for name in ("A2+", "A2-", "R4+", "R4-")},
        **{name: t0 for name in ("A3+", "A3-", "R3+", "R3-")},
        **{name: t0.at[:, :, :, :, LO] for name in ("A4+", "A4-", "R2+", "R2-")},
        **{name: sib for name in ("A5", "R1")},
        **{name: u1 for name in ("R5+", "R5-")},
        WA=wsend.at[pl.ds(0, 3)], WB=wb1.at[:, pl.ds(0, 3)], WC=wb3.at[0],
        L1=lsend, L2=lsend, L3=lsend,
    )
    for name in sent:
        assert math.prod(total[name].shape) * 2 == sent[name], name
        arrived(total[name], ss.at[AT[name]])


def copy_out(m_in, g_in, d_in, s_in, m_out, g_out, d_out, s_out, sems):
    pairs = [(m_in, m_out)]
    for i in range(4):
        cut = pl.ds(32 * i, 32)
        pairs += [(g_in.at[cut], g_out.at[cut]), (d_in.at[cut], d_out.at[cut])]
    copies = [pltpu.make_async_copy(a, b, sems.at[n]) for n, (a, b) in enumerate(pairs)]
    for copy in copies:
        copy.start()
    s_out[0] = s_in[0]
    for copy in copies:
        copy.wait()


def on_device(tokens, routes, gates, gate_up, down, expert_load, swap_pairs):
    hbm = pl.BlockSpec(memory_space=pltpu.HBM)
    vmem = pl.BlockSpec(memory_space=pltpu.VMEM)
    smem = pl.BlockSpec(memory_space=pltpu.SMEM)
    bf, f = jnp.bfloat16, jnp.float32
    sem = pltpu.SemaphoreType.DMA
    shapes = (
        jax.ShapeDtypeStruct((STEPS, ROWS, WIDE), f),
        jax.ShapeDtypeStruct((128, 16, 2 * HID), bf),
        jax.ShapeDtypeStruct((128, 16, HID), bf),
        jax.ShapeDtypeStruct((1,), f),
    )
    mixed, gu, dn, share = pl.pallas_call(
        kernel,
        out_shape=(pltpu.VMEM(shapes[0].shape, f), pltpu.VMEM(shapes[1].shape, bf), pltpu.VMEM(shapes[2].shape, bf), shapes[3]),
        in_specs=[hbm, hbm, hbm, hbm, hbm, hbm, smem],
        out_specs=(vmem, vmem, vmem, smem),
        scratch_shapes=[
            *[pltpu.VMEM((32, 16, CW), bf)] * (2 * K),
            pltpu.VMEM((K, 2, 4, 4, 16, CW), bf),
            pltpu.VMEM((K, 2, 4, 4, 16, CW), bf),
            pltpu.VMEM((K, 2, 4, 4, 16, CW), bf),
            pltpu.VMEM((STEPS, 2, 2, 4, 4, ROWS, HALF), bf),
            pltpu.VMEM((128, 16, 2 * HID), bf),
            pltpu.VMEM((128, 16, HID), bf),
            pltpu.VMEM((HB, 512, HID), bf),
            pltpu.VMEM((STEPS, 2, 2, 4, 4, ROWS, HALF), bf),
            pltpu.VMEM((STEPS, 2, 4, 4, ROWS, HALF), bf),
            pltpu.VMEM((STEPS, 2, 4, ROWS, HALF), bf),
            pltpu.VMEM((STEPS, 2, 2, 4, ROWS, HALF), bf),
            pltpu.VMEM((STEPS, 2, 4, ROWS, HALF), f),
            pltpu.VMEM((STEPS, 2, ROWS, HALF), bf),
            pltpu.VMEM((STEPS, 2, ROWS, HALF), bf),
            pltpu.VMEM((STEPS, 2, 2, ROWS, HALF), bf),
            pltpu.VMEM((STEPS, 2, 2, ROWS, HALF), bf),
            pltpu.VMEM((STEPS, TOPK, ROWS), jnp.int32),
            pltpu.VMEM((STEPS, TOPK, ROWS), f),
            pltpu.VMEM((2, 32), jnp.int32),
            pltpu.VMEM((128, 128), f),
            pltpu.VMEM((4, 4, 2, 1, 128), f),
            pltpu.VMEM((4, 4, 2, 1, 128), f),
            pltpu.VMEM((4, 4, 2, 1, 128), f),
            pltpu.VMEM((2, 4, 4, 1, 128), f),
            pltpu.VMEM((128, 128), f),
            pltpu.VMEM((8, 128), jnp.int32),
            pltpu.VMEM((4, 8, 128), jnp.int32),
            pltpu.SMEM((16,), jnp.int32),
            sem((len(STAGES),)),
            sem((K, 2, 5)),
            sem((K, 2, 2)),
            sem((STEPS, 2, 5)),
            sem((9,)),
        ],
        compiler_params=pltpu.CompilerParams(
            collective_id=0, has_side_effects=True, vmem_limit_bytes=54 * 1024 * 1024
        ),
    )(
        tokens,
        gate_up.reshape(128, 16, 2 * HID),
        down.reshape(128, 16, HID),
        routes.transpose(0, 2, 1),
        gates.transpose(0, 2, 1),
        expert_load,
        swap_pairs.T,
    )
    mixed, gu, dn = (pltpu.with_memory_space_constraint(v, pltpu.VMEM) for v in (mixed, gu, dn))
    mixed, gu, dn, share = pl.pallas_call(
        copy_out,
        out_shape=shapes,
        in_specs=[vmem, vmem, vmem, smem],
        out_specs=(hbm, hbm, hbm, smem),
        scratch_shapes=[sem((9,))],
        compiler_params=pltpu.CompilerParams(vmem_limit_bytes=4 * 1024 * 1024),
    )(mixed, gu, dn, share)
    return mixed, gu.reshape(1, WIDE, 2 * HID), dn.reshape(1, WIDE, HID), share


def solution(mesh):
    placed = (
        P(None, ("dp", "expert"), None),
        P(None, ("dp", "expert"), None),
        P(None, ("dp", "expert"), None),
        P("expert", None, None),
        P("expert", None, None),
        P("dp", None),
        P(),
    )
    return jax.shard_map(
        on_device,
        mesh=mesh,
        in_specs=placed,
        out_specs=(
            P(None, ("dp", "expert"), None),
            P("expert", None, None),
            P("expert", None, None),
            P("expert"),
        ),
        check_vma=False,
    )
```
